128 devices in a mesh: row: 16 (over y_lo, z, core), col: 8 (over y_hi, x).
Axes of the slice: x: 4, y: 4 (y_hi: 2, y_lo: 2; y = y_hi * 2 + y_lo), z: 4, core: 2. Of those that a mesh axis runs over, the one named last changes fastest.
Arguments:
- latents: bfloat16 [256, 1024, 256], P('row', 'col'), may hold values from -64 to 64
- code_ids: int32 [256, 1024], P('row', 'col'), may hold values from 0 to 16383, as said below
- norm_gain: float32 [256], replicated, may hold values from 0.1 to 1.9
- norm_bias: float32 [256], replicated, may hold values from -2 to 2
- encoder_weight: bfloat16 [3, 3, 256, 256], replicated, may hold values from -0.125 to 0.125
- codebook: bfloat16 [16384, 256], replicated, may hold values from -6 to 6
- decoder_weight: bfloat16 [3, 3, 256, 256], replicated, may hold values from -0.125 to 0.125
- decoded_cotangent: bfloat16 [256, 1024, 256], P('row', 'col'), may hold values from -6 to 6
Outputs:
- decoded: bfloat16 [256, 1024, 256], P('row', 'col')
- latents_grad: bfloat16 [256, 1024, 256], P('row', 'col')
- norm_gain_grad: float32 [256], replicated
- norm_bias_grad: float32 [256], replicated
- encoder_weight_grad: float32 [3, 3, 256, 256], replicated
- decoder_weight_grad: float32 [3, 3, 256, 256], replicated
- codebook_grad: float32 [16384, 256], P(('row', 'col'))
The draws below stay inside these ranges and needn't reach their ends.
Inputs may be any that keep to these rules, and one draw needn't show every extreme that they name: On the 16 x 128 positions of one device, at most 32 code_ids fall in any one aligned block of 128 codes; in every draw one block holds exactly 32 of them on every device.
All inputs are finite; a program needn't handle non-finite values.
Results may differ from the reference program's by a relative error of at most 0.002.
The reference program's roundings to bfloat16 on the way (of `smooth`, `quantized` and `enc_back_b`) count: a program that leaves them out, or rounds other values in their place, can miss the bound.
Values may be sent and summed in bfloat16 or wider, within the bound.
A program may use at most 128 MiB of HBM per device.

```python
import jax
import jax.numpy as jnp
from jax import lax

C = 256
K = 16384
G = 32
HT = 16
WT = 128
H = 256
W = 1024
N_ROW = 16
N_COL = 8


def draw_latents(key, part):
    height = HT * N_ROW
    breadth = WT * N_COL
    key_base, key_chan = jax.random.split(key, 2)
    centre_row = height // 2 + HT / 2.0
    row_dist = jnp.abs(jnp.arange(height, dtype=jnp.float32) + 0.5 - centre_row) / height
    row_shape = jnp.maximum(0.0, 1.0 - 4.0 * row_dist)
    col_frac = jnp.arange(breadth, dtype=jnp.float32) / max(breadth - 1, 1)
    base_draw = jnp.clip(jax.random.normal(key_base, (height, breadth, C), jnp.float32), -4.0, 4.0)
    row_scale = jnp.exp(jnp.log(10.0) * row_shape)
    chan_scale = jnp.exp(jax.random.uniform(key_chan, (C,), jnp.float32, jnp.log(0.7), jnp.log(1.4)))
    col_scale = jnp.exp(-jnp.log(3.0) * col_frac)
    scale_all = row_scale[:, None, None] * col_scale[None, :, None] * chan_scale[None, None, :]
    return (base_draw * scale_all).astype(jnp.bfloat16)


def draw_code_ids(key, part):
    devices = N_ROW * N_COL
    positions = HT * WT
    base_count = positions // devices
    block_codes = K // devices
    key_star, key_blocks = jax.random.split(jax.random.fold_in(key, 11))
    star_owner = jax.random.randint(key_star, (), 0, devices)

    def one_block(block_key):
        key_perm, key_delta, key_order, key_local = jax.random.split(block_key, 4)
        perm_owner = jax.random.permutation(key_perm, devices)
        deltas = jax.random.randint(key_delta, (devices // 2,), 0, base_count + 1).at[0].set(base_count)
        paired = jnp.stack([base_count + deltas, base_count - deltas], 1).reshape(devices)
        counts_owner = jnp.zeros((devices,), jnp.int32).at[perm_owner].set(paired.astype(jnp.int32))
        rotate_by = (star_owner - perm_owner[0]) % devices
        counts_owner = jnp.roll(counts_owner, rotate_by)
        owner_list = jnp.repeat(jnp.arange(devices, dtype=jnp.int32), counts_owner, total_repeat_length=positions)
        owner_list = jax.random.permutation(key_order, owner_list)
        local_code = jax.random.randint(key_local, (positions,), 0, block_codes)
        return (owner_list * block_codes + local_code).astype(jnp.int32).reshape(HT, WT)
    block_keys = jax.random.split(key_blocks, devices)
    blocks_all = jax.vmap(one_block)(block_keys)
    return blocks_all.reshape(N_ROW, N_COL, HT, WT).transpose(0, 2, 1, 3).reshape(HT * N_ROW, WT * N_COL)


def block_scale(own_key, shape, shards, least, high):
    loudness = 1.0
    for position, blocks in shards:
        heights = jax.random.uniform(jax.random.fold_in(jax.random.fold_in(own_key, 6), position), (blocks,), jnp.float32, least / len(shards), high / len(shards))
        loudness = loudness * jnp.repeat(jnp.exp(heights), shape[position] // blocks).reshape((-1,) + (1,) * (len(shape) - 1 - position))
    return loudness


def normal_values(own_key, shape, width, bound, cuts=(), kind=jnp.bfloat16):
    gain = block_scale(own_key, shape, cuts, -0.22, 0.18) if cuts else 1.0
    result = jax.random.normal(own_key, shape, jnp.float32) * width * gain
    return jnp.minimum(jnp.maximum(result, -bound), bound).astype(kind)


def setup_inputs(seed: int = 0) -> dict:
    key_of = jax.random.split(jax.random.key(seed), 9)
    return {
        "latents": draw_latents(jax.random.fold_in(key_of[8], 71), 0),
        "code_ids": draw_code_ids(jax.random.fold_in(key_of[8], 71), 0),
        "norm_gain": jnp.clip(1.0 + 0.18 * jax.random.normal(key_of[2], (C,), jnp.float32), 0.1, 1.9),
        "norm_bias": normal_values(key_of[3], (C,), 0.5, 2.0, (), jnp.float32),
        "encoder_weight": normal_values(key_of[4], (3, 3, C, C), (9 * C) ** -0.5, 0.125),
        "codebook": normal_values(key_of[5], (K, C), 1.0, 6.0),
        "decoder_weight": normal_values(key_of[6], (3, 3, C, C), (9 * C) ** -0.5, 0.125),
        "decoded_cotangent": normal_values(key_of[7], (H, W, C), 1.0, 6.0, ((0, 16), (1, 8))),
    }


epsilon = 1e-06
commit_beta = 0.25

def conv_forward(inputs, weight):
    height = inputs.shape[0]
    breadth = inputs.shape[1]
    padded = jnp.pad(inputs.astype(jnp.float32), ((1, 1), (1, 1), (0, 0)))
    weight_float = weight.astype(jnp.float32)
    summed = jnp.zeros((height, breadth, weight.shape[3]), jnp.float32)
    for shift_r in range(3):
        for shift_c in range(3):
            window = padded[shift_r:shift_r + height, shift_c:shift_c + breadth]
            summed = summed + jnp.einsum('hwi,io->hwo', window, weight_float[shift_r, shift_c])
    return summed

def conv_back(grads, weight):
    height = grads.shape[0]
    breadth = grads.shape[1]
    padded = jnp.pad(grads.astype(jnp.float32), ((1, 1), (1, 1), (0, 0)))
    weight_float = weight.astype(jnp.float32)
    summed = jnp.zeros((height, breadth, weight.shape[2]), jnp.float32)
    for shift_r in range(3):
        for shift_c in range(3):
            window = padded[2 - shift_r:2 - shift_r + height, 2 - shift_c:2 - shift_c + breadth]
            summed = summed + jnp.einsum('hwo,io->hwi', window, weight_float[shift_r, shift_c])
    return summed

def weight_grad(inputs, grads):
    height = inputs.shape[0]
    breadth = inputs.shape[1]
    padded = jnp.pad(inputs.astype(jnp.float32), ((1, 1), (1, 1), (0, 0)))
    grads_float = grads.astype(jnp.float32)
    pieces = []
    for shift_r in range(3):
        for shift_c in range(3):
            window = padded[shift_r:shift_r + height, shift_c:shift_c + breadth]
            pieces.append(jnp.einsum('hwi,hwo->io', window, grads_float))
    stacked = jnp.stack(pieces)
    return stacked.reshape(3, 3, stacked.shape[1], stacked.shape[2])

def rotate_back(encoded, embed, back):
    z_norm = jnp.sqrt(lax.optimization_barrier(jnp.sum(encoded * encoded, -1, keepdims=True)) + epsilon)
    e_norm = jnp.sqrt(lax.optimization_barrier(jnp.sum(embed * embed, -1, keepdims=True)) + epsilon)
    z_unit = encoded / z_norm
    e_unit = embed / e_norm
    mirror = z_unit + e_unit
    mirror = mirror / jnp.sqrt(lax.optimization_barrier(jnp.sum(mirror * mirror, -1, keepdims=True)) + epsilon)
    stretch = e_norm / z_norm
    along_mirror = lax.optimization_barrier(jnp.sum(mirror * back, -1, keepdims=True))
    along_code = lax.optimization_barrier(jnp.sum(e_unit * back, -1, keepdims=True))
    turned = back - 2.0 * mirror * along_mirror + 2.0 * z_unit * along_code
    return stretch * turned + commit_beta * (encoded - embed)

def reference(latents, code_ids, norm_gain, norm_bias, encoder_weight, codebook, decoder_weight, decoded_cotangent):
    channels = latents.shape[2]
    per_group = channels // G
    group_count = H * W * per_group
    xfloat = latents.astype(jnp.float32)
    mean_group = lax.optimization_barrier(jnp.sum(xfloat, (0, 1))).reshape(G, per_group).sum(1) / group_count
    centered = xfloat - jnp.repeat(mean_group, per_group)
    var_group = lax.optimization_barrier(jnp.sum(centered * centered, (0, 1))).reshape(G, per_group).sum(1) / group_count
    inv_std = jnp.repeat(lax.rsqrt(var_group + epsilon), per_group)
    normed = centered * inv_std
    act = normed * norm_gain + norm_bias
    smooth = jax.nn.silu(act).astype(jnp.bfloat16)
    encoded = xfloat + conv_forward(smooth, encoder_weight)
    quantized = codebook[code_ids]
    decoded = conv_forward(quantized, decoder_weight).astype(jnp.bfloat16)
    back_quant = conv_back(decoded_cotangent, decoder_weight)
    decoder_weight_grad = weight_grad(quantized, decoded_cotangent)
    embed = quantized.astype(jnp.float32)
    enc_back = rotate_back(encoded, embed, back_quant)
    enc_back_b = enc_back.astype(jnp.bfloat16)
    code_pull = K / (H * W) * (embed - encoded)
    codebook_grad = jnp.zeros((K, channels), jnp.float32).at[code_ids.reshape(-1)].add(code_pull.reshape(-1, channels))
    back_smooth = conv_back(enc_back_b, encoder_weight)
    encoder_weight_grad = weight_grad(smooth, enc_back_b)
    sigmoid_act = jax.nn.sigmoid(act)
    back_act = back_smooth * sigmoid_act * (1.0 + act * (1.0 - sigmoid_act))
    norm_bias_grad = lax.optimization_barrier(jnp.sum(back_act, (0, 1)))
    norm_gain_grad = lax.optimization_barrier(jnp.sum(back_act * normed, (0, 1)))
    first_mean = jnp.repeat((norm_gain * norm_bias_grad).reshape(G, per_group).sum(1) / group_count, per_group)
    second_mean = jnp.repeat((norm_gain * norm_gain_grad).reshape(G, per_group).sum(1) / group_count, per_group)
    latents_grad = (inv_std * (back_act * norm_gain - first_mean - normed * second_mean) + enc_back).astype(jnp.bfloat16)
    return (decoded, latents_grad, norm_gain_grad, norm_bias_grad, encoder_weight_grad, decoder_weight_grad, codebook_grad)
```

```python
import functools

import jax
import jax.numpy as jnp
from jax import lax
from jax.experimental import pallas as pl
from jax.experimental.pallas import tpu as pltpu
from jax.sharding import PartitionSpec as P

G = 32
NR, NC = 16, 8
N = NR * NC
HT, WT, C = 16, 128, 256
POS = HT * WT
CAP = 32
epsilon = 1e-06
commit_beta = 0.25
f32, bf16, i32 = jnp.float32, jnp.bfloat16, jnp.int32
MESH = pl.DeviceIdType.MESH
VM = pl.BlockSpec(memory_space=pltpu.VMEM)
SM = pl.BlockSpec(memory_space=pltpu.SMEM)
ANY = pl.BlockSpec(memory_space=pl.ANY)
NT = (((1,), (1,)), ((), ()))
STAGE = 1024


def iota(shape, dim):
    return lax.broadcasted_iota(i32, shape, dim)


def gather_kernel(ids_s, ids_v, cb, q_out, qt_out, slot_out, idrow_out, cbf, stage, qf, sems):
    parts = cb.shape[0] // STAGE

    def fetch(c, slot):
        return pltpu.make_async_copy(
            cb.at[pl.ds(pl.multiple_of(c * STAGE, STAGE), STAGE)], stage.at[slot], sems.at[slot]
        )

    fetch(0, 0).start()
    fetch(1, 1).start()
    upper = (iota((WT, WT), 0) < iota((WT, WT), 1)).astype(f32).astype(bf16)
    base = jnp.zeros((N, 1), f32)
    named = jnp.zeros((N, WT), f32)
    for h in range(HT):
        row = ids_v[h : h + 1, :]
        member = (iota((N, WT), 0) == (row >> 7)).astype(f32)
        member_b = member.astype(bf16)
        ahead = jnp.dot(member_b, upper, preferred_element_type=f32)
        slot = jnp.sum(member * (ahead + base), axis=0, keepdims=True)
        base = base + jnp.sum(member, axis=1, keepdims=True)
        slot_out[h : h + 1, :] = slot
        local = ((row & 127) + 1).astype(f32)
        lanes = (iota((WT, WT), 0) & (CAP - 1)).astype(f32)
        spread = jnp.where(lanes == slot, local, 0.0).astype(bf16)
        named = named + lax.dot_general(member_b, spread, NT, preferred_element_type=f32)
    idrow_out[:, 0, :] = named - 1.0

    def convert(c, carry):
        slot = lax.rem(c, 2)
        fetch(c, slot).wait()
        for k in range(STAGE // 128):
            cbf[pl.ds(pl.multiple_of(c * STAGE + k * 128, 128), 128), :] = stage[
                slot, k * 128 : (k + 1) * 128, :
            ].astype(f32)

        @pl.when(c + 2 < parts)
        def _():
            fetch(c + 2, slot).start()

        return carry

    lax.fori_loop(0, parts, convert, 0)

    def pick(t, carry):
        h = t // 8
        x = lax.rem(t, 8) * 16
        for j in range(16):
            qf[pl.ds(pl.multiple_of(t * 16, 16) + j, 1), :] = cbf[pl.ds(ids_s[h, x + j], 1), :]
        return carry

    lax.fori_loop(0, POS // 16, pick, 0)

    def finish(h, carry):
        v = qf[pl.ds(pl.multiple_of(h * WT, WT), WT), :]
        q_out[h] = v.astype(bf16)
        qt_out[:, pl.ds(pl.multiple_of(h * WT, WT), WT)] = v.T.astype(bf16)
        return carry

    lax.fori_loop(0, HT, finish, 0)


def gather(code_ids, codebook):
    return pl.pallas_call(
        gather_kernel,
        out_shape=(
            jax.ShapeDtypeStruct((HT, WT, C), bf16),
            jax.ShapeDtypeStruct((C, POS), bf16),
            jax.ShapeDtypeStruct((HT, WT), f32),
            jax.ShapeDtypeStruct((N, 1, WT), f32),
        ),
        in_specs=[SM, VM, ANY],
        out_specs=(VM, VM, VM, VM),
        scratch_shapes=[
            pltpu.VMEM((codebook.shape[0], C), f32),
            pltpu.VMEM((2, STAGE, C), bf16),
            pltpu.VMEM((POS, C), f32),
            pltpu.SemaphoreType.DMA((2,)),
        ],
        compiler_params=pltpu.CompilerParams(vmem_limit_bytes=40 << 20),
        name="gather",
    )(code_ids, code_ids, codebook)


COT, QNT, SMO, BCK = 0, 1, 2, 3


def main_kernel(
    lat, ids_v, slots, idrow, gain, bias, w_enc, w_dec, q, qt, cot,
    dec_out, lg_out, gsum_out, wg_out, cg_out,
    S_a, S_q, S_s, hr, hc, hs, colf, cf,
    bq, enc, eb, ba, pull, st,
    msg, stat, sb, rb, idr, dkey, skey,
    grad, p0r, rss, rsr, zr, ag,
    h_send, h_recv, s_send, s_recv, i_send, i_recv, c_send, c_recv, g_send, g_recv,
):
    row, col = lax.axis_index("row"), lax.axis_index("col")
    me = row * NC + col
    core = lax.rem(row, 2)
    zed = lax.rem(row // 2, 4)
    ylo = row // 8
    plane = ylo * 8 + col
    up, dn = lax.rem(row + NR - 1, NR), lax.rem(row + 1, NR)
    lf, rt = lax.rem(col + NC - 1, NC), lax.rem(col + 1, NC)
    count = float(HT * WT * N * (C // G))

    barrier = pltpu.get_barrier_semaphore()

    def peer(j):
        t = lax.rem(me + j, N)
        return t, {"row": t // NC, "col": lax.rem(t, NC)}

    def hello(j, carry):
        pl.semaphore_signal(barrier, inc=1, device_id=peer(j)[1], device_id_type=MESH)
        return carry

    lax.fori_loop(1, N, hello, 0)

    def remote(src, dst, ss, rs, dev):
        return pltpu.make_async_remote_copy(
            src_ref=src, dst_ref=dst, send_sem=ss, recv_sem=rs, device_id=dev, device_id_type=MESH
        )

    def drain(ref, sem):
        pltpu.make_async_copy(ref, ref, sem).wait()

    def halo_copies(f, S):
        here = {
            0: (S.at[1, HT], hr.at[f, 0], dn, col),
            1: (S.at[1, 1], hr.at[f, 1], up, col),
            2: (hs.at[f, 1], hc.at[f, 1], row, rt),
            3: (hs.at[f, 1], hc.at[f, 0], dn, rt),
            4: (hs.at[f, 1], hc.at[f, 2], up, rt),
            5: (hs.at[f, 0], hc.at[f, 4], row, lf),
            6: (hs.at[f, 0], hc.at[f, 3], dn, lf),
            7: (hs.at[f, 0], hc.at[f, 5], up, lf),
        }
        return [
            remote(s, d, h_send.at[f, k], h_recv.at[f, k], {"row": r, "col": c})
            for k, (s, d, r, c) in here.items()
        ]

    def halo_send(f, S):
        hs[f] = colf[...].astype(bf16)
        for copy in halo_copies(f, S):
            copy.start()

    ok_u = jnp.where(row > 0, 1.0, 0.0).astype(f32)
    ok_d = jnp.where(row < NR - 1, 1.0, 0.0).astype(f32)
    ok_l = jnp.where(col > 0, 1.0, 0.0).astype(f32)
    ok_r = jnp.where(col < NC - 1, 1.0, 0.0).astype(f32)

    def halo_finish(f, S):
        for copy in halo_copies(f, S):
            copy.wait()
        S[1, 0] = (hr[f, 0].astype(f32) * ok_u).astype(bf16)
        S[1, HT + 1] = (hr[f, 1].astype(f32) * ok_d).astype(bf16)
        for side, ok in ((0, ok_l), (1, ok_r)):
            above = hc[f, 3 * side].astype(f32) * (ok * ok_u)
            below = hc[f, 3 * side + 2].astype(f32) * (ok * ok_d)
            cf[side, 8:24] = hc[f, 3 * side + 1].astype(f32) * ok
            cf[side, 7:8] = above[15:16]
            cf[side, 24:25] = below[0:1]

        def shift(hh, carry):
            v = S[1, hh].astype(f32)
            place = iota((WT, C), 0)
            S[0, hh] = jnp.where(place == 0, cf[0, pl.ds(hh + 7, 1)], pltpu.roll(v, 1, 0)).astype(bf16)
            S[2, hh] = jnp.where(
                place == WT - 1, cf[1, pl.ds(hh + 7, 1)], pltpu.roll(v, WT - 1, 0)
            ).astype(bf16)
            return carry

        lax.fori_loop(0, HT + 2, shift, 0)

    def take_cols(h, v):
        colf[0, pl.ds(h, 1)] = v[0:1]
        colf[1, pl.ds(h, 1)] = v[WT - 1 : WT]

    def load_field(S, src):
        def body(h, carry):
            v = src[h]
            S[1, h + 1] = v
            take_cols(h, v.astype(f32))
            return carry

        lax.fori_loop(0, HT, body, 0)

    RB = 4

    def windows(S, r0, flip):
        parts = []
        for dy in range(3):
            for dx in range(3):
                a, b = (2 - dx, 2 - dy) if flip else (dx, dy)
                parts.append(S[a, pl.ds(r0 + b, RB)].reshape(RB * WT, C))
        return jnp.concatenate(parts, axis=1)

    def conv(S, w, use):
        def body(i, carry):
            r0 = i * RB
            use(r0, jnp.dot(windows(S, r0, False), w[...].reshape(9 * C, C), preferred_element_type=f32))
            return carry

        lax.fori_loop(0, HT // RB, body, 0)

    def convt(S, w, use):
        def body(i, carry):
            r0 = i * RB
            wide = jnp.concatenate([w[k] for k in range(9)], axis=1)
            use(r0, lax.dot_general(windows(S, r0, True), wide, NT, preferred_element_type=f32))
            return carry

        lax.fori_loop(0, HT // RB, body, 0)

    def wgrad(g, ut, S):
        def body(k, carry):
            dy, dx = k // 3, lax.rem(k, 3)
            win = S[2 - dx, pl.ds(2 - dy, HT)].reshape(POS, C)
            res = jnp.dot(ut[...], win, preferred_element_type=f32)
            at = pl.ds(pl.multiple_of(k * C, C), C)
            grad[g, 0, at, :] = res[:, :128]
            grad[g, 1, at, :] = res[:, 128:]
            return carry

        lax.fori_loop(0, 9, body, 0)

    partner = {"row": row + 1 - 2 * core, "col": col}

    def plane_peer(j):
        t = lax.rem(plane + j, 16)
        return t, {"row": (t // 8) * 8 + lax.rem(row, 8), "col": lax.rem(t, 8)}

    def pair0(g):
        return remote(grad.at[g, 1 - core], p0r.at[g], g_send.at[g, 0], g_recv.at[g, 0], partner)

    def ar0(g):
        pair0(g).start()

    def ar1(g):
        pair0(g).wait()

        def add(j, carry):
            at = pl.ds(pl.multiple_of(j * 144, 16), 144)
            rss[g, j] = grad[g, core, at, :] + p0r[g, at, :]
            return carry

        lax.fori_loop(0, 16, add, 0)
        rsr[g, plane] = rss[g, plane]

        def send(j, carry):
            t, dev = plane_peer(j)
            remote(rss.at[g, t], rsr.at[g, plane], g_send.at[g, 1], g_recv.at[g, 1], dev).start()
            return carry

        lax.fori_loop(1, 16, send, 0)

    def ar2(g):
        drain(rss.at[g, pl.ds(0, 15)], g_send.at[g, 1])
        drain(rsr.at[g, pl.ds(0, 15)], g_recv.at[g, 1])
        total = rsr[g, 0]
        for j in range(1, 16):
            total = total + rsr[g, j]
        zr[g, zed] = total

        def send(j, carry):
            t = lax.rem(zed + j, 4)
            dev = {"row": ylo * 8 + t * 2 + core, "col": col}
            remote(zr.at[g, zed], zr.at[g, zed], g_send.at[g, 2], g_recv.at[g, 2], dev).start()
            return carry

        lax.fori_loop(1, 4, send, 0)

    def ar3(g):
        drain(zr.at[g, pl.ds(0, 3)], g_send.at[g, 2])
        drain(zr.at[g, pl.ds(0, 3)], g_recv.at[g, 2])
        ag[g, core, plane] = ((zr[g, 0] + zr[g, 1]) + (zr[g, 2] + zr[g, 3])).astype(bf16)

        def send(j, carry):
            _, dev = plane_peer(j)
            mine = ag.at[g, core, plane]
            remote(mine, mine, g_send.at[g, 3], g_recv.at[g, 3], dev).start()
            return carry

        lax.fori_loop(1, 16, send, 0)

    def pair4(g):
        mine = ag.at[g, core]
        return remote(mine, mine, g_send.at[g, 4], g_recv.at[g, 4], partner)

    def ar4(g):
        drain(ag.at[g, 0, pl.ds(0, 15)], g_send.at[g, 3])
        drain(ag.at[g, 0, pl.ds(0, 15)], g_recv.at[g, 3])
        pair4(g).start()

    def ar5(g):
        pair4(g).wait()
        wg_out[g] = ag[g]

    def sum_send(a):
        stat[a, me] = msg[a]

        def send(j, carry):
            remote(msg.at[a], stat.at[a, me], s_send.at[a], s_recv.at[a], peer(j)[1]).start()
            return carry

        lax.fori_loop(1, N, send, 0)

    def sum_finish(a):
        drain(stat.at[a, pl.ds(0, N - 1)], s_send.at[a])
        drain(stat.at[a, pl.ds(0, N - 1)], s_recv.at[a])
        return jnp.sum(stat[a], axis=0)

    same = (iota((C, C), 0) // (C // G) == iota((C, C), 1) // (C // G)).astype(f32)

    def per_group(v):
        wide = jnp.concatenate([v, jnp.zeros((6, C), f32)], axis=0)
        return jnp.dot(wide, same, precision=lax.Precision.HIGHEST, preferred_element_type=f32)

    def first(h, carry):
        v = lat[h].astype(f32)
        return carry[0] + jnp.sum(v, 0, keepdims=True), carry[1] + jnp.sum(v * v, 0, keepdims=True)

    zero = jnp.zeros((1, C), f32)
    s1, s2 = lax.fori_loop(0, HT, first, (zero, zero))
    msg[0, 0:1] = s1
    msg[0, 1:2] = s2

    load_field(S_a, cot)
    pl.semaphore_wait(barrier, N - 1)
    sum_send(0)
    halo_send(COT, S_a)
    load_field(S_q, q)
    halo_send(QNT, S_q)

    def ids_send(j, carry):
        t, dev = peer(j)
        remote(idrow.at[t], idr.at[me], i_send.at[0], i_recv.at[0], dev).start()
        return carry

    lax.fori_loop(1, N, ids_send, 0)
    idr[me] = idrow[me]

    halo_finish(COT, S_a)

    def keep_bq(r0, v):
        bq[pl.ds(r0, RB)] = v.reshape(RB, WT, C)

    convt(S_a, w_dec, keep_bq)
    wgrad(0, qt, S_a)
    ar0(0)

    tot = sum_finish(0)
    grp = per_group(tot)
    mean = grp[0:1] / count
    var = grp[1:2] / count - mean * mean
    inv = lax.rsqrt(var + epsilon)
    gain_v, bias_v = gain[...], bias[...]

    def smoothing(h, carry):
        act = (lat[h].astype(f32) - mean) * inv * gain_v + bias_v
        v = act * jax.nn.sigmoid(act)
        S_s[1, h + 1] = v.astype(bf16)
        st[:, pl.ds(pl.multiple_of(h * WT, WT), WT)] = v.T.astype(bf16)
        take_cols(h, v)
        return carry

    lax.fori_loop(0, HT, smoothing, 0)
    halo_send(SMO, S_s)
    ar1(0)
    halo_finish(QNT, S_q)

    def keep_dec(r0, v):
        dec_out[pl.ds(r0, RB)] = v.reshape(RB, WT, C).astype(bf16)

    halo_finish(SMO, S_s)

    def keep_enc(r0, v):
        enc[pl.ds(r0, RB)] = v.reshape(RB, WT, C) + lat[pl.ds(r0, RB)].astype(f32)

    conv(S_s, w_enc, keep_enc)
    ar2(0)

    code_scale = float(16384) / (HT * WT * N)

    def rotate(h, carry):
        for k in range(4):
            at = slice(k * 32, (k + 1) * 32)
            z, e, b = enc[h, at], q[h, at].astype(f32), bq[h, at]
            z_norm = jnp.sqrt(jnp.sum(z * z, -1, keepdims=True) + epsilon)
            e_norm = jnp.sqrt(jnp.sum(e * e, -1, keepdims=True) + epsilon)
            z_unit = z * (1.0 / z_norm)
            e_unit = e * (1.0 / e_norm)
            mirror = z_unit + e_unit
            mirror = mirror * (1.0 / jnp.sqrt(jnp.sum(mirror * mirror, -1, keepdims=True) + epsilon))
            along_mirror = jnp.sum(mirror * b, -1, keepdims=True)
            along_code = jnp.sum(e_unit * b, -1, keepdims=True)
            turned = b - (2.0 * along_mirror) * mirror + (2.0 * along_code) * z_unit
            back = (e_norm / z_norm) * turned + commit_beta * (z - e)
            eb[h, at] = back
            S_a[1, h + 1, at] = back.astype(bf16)
            pull[pl.ds(pl.multiple_of(h * WT + k * 32, 32), 32), :] = (code_scale * (e - z)).astype(bf16)
            if k == 0:
                colf[0, pl.ds(h, 1)] = back[0:1]
            if k == 3:
                colf[1, pl.ds(h, 1)] = back[31:32]
        return carry

    lax.fori_loop(0, HT, rotate, 0)
    halo_send(BCK, S_a)
    ar3(0)

    for h in range(HT):
        at = slice(h * WT, (h + 1) * WT)
        dkey[:, at] = jnp.broadcast_to((ids_v[h : h + 1, :] >> 7).astype(f32), (16, WT)).astype(bf16)
        skey[:, at] = jnp.broadcast_to(slots[h : h + 1, :], (16, WT)).astype(bf16)
    low = iota((16, POS), 0).astype(f32).astype(bf16)
    one, nil, gone = jnp.ones((16, POS), bf16), jnp.zeros((16, POS), bf16), jnp.full((16, POS), -1.0, bf16)

    def pack(i, carry):
        first_owner = lax.rem(me // 8 + i, N // 8) * 8
        parts = []
        for j in range(8):
            owner = jnp.full((16, POS), (first_owner + j).astype(f32), f32).astype(bf16)
            key = jnp.where(dkey[...] == owner, skey[...], gone)
            parts.append(jnp.where(key == low, one, nil))
            parts.append(jnp.where(key == low + 16.0, one, nil))
        select = jnp.concatenate(parts, axis=0)
        rows = jnp.dot(select, pull[...], preferred_element_type=f32)
        sb[pl.ds(first_owner, 8)] = rows.reshape(8, CAP, C).astype(bf16)
        return carry

    lax.fori_loop(0, N // 8, pack, 0)

    def rows_send(j, carry):
        t, dev = peer(j)
        remote(sb.at[t], rb.at[me], c_send.at[0], c_recv.at[0], dev).start()
        return carry

    lax.fori_loop(1, N, rows_send, 0)
    rb[me] = sb[me]

    halo_finish(BCK, S_a)
    wgrad(1, st, S_a)
    ar0(1)
    ar4(0)

    def backward(r0, v):
        bs = v.reshape(RB, WT, C)
        s_b, s_g = zero, zero
        for k in range(RB):
            normed = (lat[r0 + k].astype(f32) - mean) * inv
            act = normed * gain_v + bias_v
            s = jax.nn.sigmoid(act)
            t = bs[k] * s * (1.0 + act * (1.0 - s))
            ba[r0 + k] = t
            s_b = s_b + jnp.sum(t, 0, keepdims=True)
            s_g = s_g + jnp.sum(t * normed, 0, keepdims=True)
        msg[1, 0:1] += s_b
        msg[1, 1:2] += s_g

    msg[1] = jnp.zeros((2, C), f32)
    convt(S_a, w_enc, backward)
    sum_send(1)
    ar1(1)
    ar5(0)
    conv(S_q, w_dec, keep_dec)
    ar2(1)

    tot2 = sum_finish(1)
    gsum_out[...] = tot2
    means = per_group(tot2 * gain_v) * (1.0 / count)
    mean1, mean2 = means[0:1], means[1:2]

    def last(h, carry):
        normed = (lat[h].astype(f32) - mean) * inv
        lg_out[h] = (inv * (ba[h] * gain_v - mean1 - normed * mean2) + eb[h]).astype(bf16)
        return carry

    lax.fori_loop(0, HT, last, 0)
    ar3(1)

    drain(idr.at[pl.ds(0, N - 1)], i_send.at[0])
    drain(idr.at[pl.ds(0, N - 1)], i_recv.at[0])
    drain(sb.at[pl.ds(0, N - 1)], c_send.at[0])
    drain(rb.at[pl.ds(0, N - 1)], c_recv.at[0])
    quarter = iota((1, WT), 1) // CAP

    def collect(g, acc):
        hot = []
        for half in range(2):
            names = idr[g * 8 + half * 4]
            for j in range(1, 4):
                names = jnp.where(quarter == j, idr[g * 8 + half * 4 + j], names)
            hot.append((iota((N, WT), 0).astype(f32) == names).astype(f32).astype(bf16))
        rows = rb[pl.ds(g * 8, 8)].reshape(8 * CAP, C)
        return acc + jnp.dot(jnp.concatenate(hot, axis=1), rows, preferred_element_type=f32)

    cg_out[...] = lax.fori_loop(0, N // 8, collect, jnp.zeros((N, C), f32))
    ar4(1)
    ar5(1)


def main(lat, code_ids, slots, idrow, gain, bias, w_enc, w_dec, q, qt, cot):
    dma = pltpu.SemaphoreType.DMA
    V = pltpu.VMEM
    field = V((3, HT + 2, WT, C), bf16)
    tile = V((HT, WT, C), f32)
    return pl.pallas_call(
        main_kernel,
        out_shape=(
            jax.ShapeDtypeStruct((HT, WT, C), bf16),
            jax.ShapeDtypeStruct((HT, WT, C), bf16),
            jax.ShapeDtypeStruct((2, C), f32),
            jax.ShapeDtypeStruct((2, 2, 16, 144, 128), bf16),
            jax.ShapeDtypeStruct((N, C), f32),
        ),
        in_specs=[VM] * 11,
        out_specs=(VM,) * 5,
        scratch_shapes=[
            field, field, field,
            V((4, 2, WT, C), bf16), V((4, 6, HT, C), bf16), V((4, 2, HT, C), bf16),
            V((2, HT, C), f32), V((2, 32, C), f32),
            tile, tile, tile, tile, V((POS, C), bf16), V((C, POS), bf16),
            V((2, 2, C), f32), V((2, N, 2, C), f32),
            V((N, CAP, C), bf16), V((N, CAP, C), bf16), V((N, 1, WT), f32),
            V((16, POS), bf16), V((16, POS), bf16),
            V((2, 2, 9 * C, 128), f32), V((2, 9 * C, 128), f32),
            V((2, 16, 144, 128), f32), V((2, 16, 144, 128), f32),
            V((2, 4, 144, 128), f32), V((2, 2, 16, 144, 128), bf16),
            dma((4, 8)), dma((4, 8)), dma((2,)), dma((2,)), dma((1,)), dma((1,)), dma((1,)), dma((1,)),
            dma((2, 5)), dma((2, 5)),
        ],
        compiler_params=pltpu.CompilerParams(
            collective_id=0, has_side_effects=True, vmem_limit_bytes=66_000_000
        ),
        name="main",
    )(lat, code_ids, slots, idrow, gain, bias, w_enc, w_dec, q, qt, cot)


def body(latents, code_ids, norm_gain, norm_bias, encoder_weight, codebook, decoder_weight, cotangent):
    q, qt, slots, idrow = gather(code_ids, codebook)
    decoded, latents_grad, gsum, wg, cg = main(
        latents, code_ids, slots, idrow, norm_gain.reshape(1, C), norm_bias.reshape(1, C),
        encoder_weight.reshape(9, C, C), decoder_weight.reshape(9, C, C), q, qt, cotangent,
    )
    wg = wg.reshape(2, 2, 9 * C, 128).transpose(0, 2, 1, 3).reshape(2, 3, 3, C, C).astype(f32)
    return decoded, latents_grad, gsum[1], gsum[0], wg[1], wg[0], cg


def solution(mesh):
    tiled = P("row", "col", None)
    in_specs = (tiled, P("row", "col"), P(), P(), P(), P(), P(), tiled)
    out_specs = (tiled, tiled, P(), P(), P(), P(), P(("row", "col"), None))
    return jax.shard_map(body, mesh=mesh, in_specs=in_specs, out_specs=out_specs, check_vma=False)
```

```python
import functools

import jax
import jax.numpy as jnp
from jax import lax
from jax.experimental import pallas as pl
from jax.experimental.pallas import tpu as pltpu
from jax.sharding import PartitionSpec as P

G = 32
NR, NC = 16, 8
N = NR * NC
HT, WT, C = 16, 128, 256
POS = HT * WT
CAP = 32
epsilon = 1e-06
commit_beta = 0.25
f32, bf16, i32 = jnp.float32, jnp.bfloat16, jnp.int32
MESH = pl.DeviceIdType.MESH
VM = pl.BlockSpec(memory_space=pltpu.VMEM)
SM = pl.BlockSpec(memory_space=pltpu.SMEM)
ANY = pl.BlockSpec(memory_space=pl.ANY)
NT = (((1,), (1,)), ((), ()))
STAGE = 1024


def iota(shape, dim):
    return lax.broadcasted_iota(i32, shape, dim)


COT, QNT, SMO, BCK = 0, 1, 2, 3


def main_kernel(
    lat, ids_s, ids_v, gain, bias, w_enc_hbm, w_dec_hbm, cot_hbm, cb,
    dec_out, lg_out, gsum_out, wg_out, cg_out,
    S_a, S_q, S_s, hr, hc, hs, colf, cf,
    cbf, stage, qf, slots, idrow, qt, w_enc, w_dec, pull, st,
    msg, stat, sb, rb, idr, dkey, skey,
    grad, p0r, rss, rsr, tb, tr, zr, ag,
    l_sems, h_send, h_recv, s_send, s_recv, i_send, i_recv, c_send, c_recv, g_send, g_recv,
):
    row, col = lax.axis_index("row"), lax.axis_index("col")
    me = row * NC + col
    core = lax.rem(row, 2)
    zed = lax.rem(row // 2, 4)
    ylo = row // 8
    up, dn = lax.rem(row + NR - 1, NR), lax.rem(row + 1, NR)
    lf, rt = lax.rem(col + NC - 1, NC), lax.rem(col + 1, NC)
    count = float(HT * WT * N * (C // G))

    barrier = pltpu.get_barrier_semaphore()

    def peer(j):
        t = lax.rem(me + j, N)
        return t, {"row": t // NC, "col": lax.rem(t, NC)}

    def hello(j, carry):
        pl.semaphore_signal(barrier, inc=1, device_id=peer(j)[1], device_id_type=MESH)
        return carry

    lax.fori_loop(1, N, hello, 0)

    def remote(src, dst, ss, rs, dev):
        return pltpu.make_async_remote_copy(
            src_ref=src, dst_ref=dst, send_sem=ss, recv_sem=rs, device_id=dev, device_id_type=MESH
        )

    def drain(ref, sem):
        pltpu.make_async_copy(ref, ref, sem).wait()

    def halo_copies(f, S):
        here = {
            0: (S.at[1, HT], hr.at[f, 0], dn, col),
            1: (S.at[1, 1], hr.at[f, 1], up, col),
            2: (hs.at[f, 1], hc.at[f, 1], row, rt),
            3: (hs.at[f, 1], hc.at[f, 0], dn, rt),
            4: (hs.at[f, 1], hc.at[f, 2], up, rt),
            5: (hs.at[f, 0], hc.at[f, 4], row, lf),
            6: (hs.at[f, 0], hc.at[f, 3], dn, lf),
            7: (hs.at[f, 0], hc.at[f, 5], up, lf),
        }
        return [
            remote(s, d, h_send.at[f, k], h_recv.at[f, k], {"row": r, "col": c})
            for k, (s, d, r, c) in here.items()
        ]

    def halo_send(f, S):
        hs[f] = colf[...].astype(bf16)
        for copy in halo_copies(f, S):
            copy.start()

    ok_u = jnp.where(row > 0, 1.0, 0.0).astype(f32)
    ok_d = jnp.where(row < NR - 1, 1.0, 0.0).astype(f32)
    ok_l = jnp.where(col > 0, 1.0, 0.0).astype(f32)
    ok_r = jnp.where(col < NC - 1, 1.0, 0.0).astype(f32)

    def halo_finish(f, S):
        for copy in halo_copies(f, S):
            copy.wait()
        S[1, 0] = (hr[f, 0].astype(f32) * ok_u).astype(bf16)
        S[1, HT + 1] = (hr[f, 1].astype(f32) * ok_d).astype(bf16)
        for side, ok in ((0, ok_l), (1, ok_r)):
            above = hc[f, 3 * side].astype(f32) * (ok * ok_u)
            below = hc[f, 3 * side + 2].astype(f32) * (ok * ok_d)
            cf[side, 8:24] = hc[f, 3 * side + 1].astype(f32) * ok
            cf[side, 7:8] = above[15:16]
            cf[side, 24:25] = below[0:1]

        def shift(hh, carry):
            v = S[1, hh].astype(f32)
            place = iota((WT, C), 0)
            S[0, hh] = jnp.where(place == 0, cf[0, pl.ds(hh + 7, 1)], pltpu.roll(v, 1, 0)).astype(bf16)
            S[2, hh] = jnp.where(
                place == WT - 1, cf[1, pl.ds(hh + 7, 1)], pltpu.roll(v, WT - 1, 0)
            ).astype(bf16)
            return carry

        lax.fori_loop(0, HT + 2, shift, 0)

    def take_cols(h, v):
        colf[0, pl.ds(h, 1)] = v[0:1]
        colf[1, pl.ds(h, 1)] = v[WT - 1 : WT]

    def field_cols(S):
        def body(h, carry):
            take_cols(h, S[1, h + 1].astype(f32))
            return carry

        lax.fori_loop(0, HT, body, 0)

    BQ, ENC, EB, BA = 0, POS, 2 * POS, 3 * POS

    def put(plane, r0, v):
        cbf[pl.ds(pl.multiple_of(plane + r0 * WT, WT), v.shape[0]), :] = v

    def row_of(plane, h):
        return cbf[pl.ds(pl.multiple_of(plane + h * WT, WT), WT), :]

    RB = 4

    def windows(S, r0, flip):
        parts = []
        for dy in range(3):
            for dx in range(3):
                a, b = (2 - dx, 2 - dy) if flip else (dx, dy)
                parts.append(S[a, pl.ds(r0 + b, RB)].reshape(RB * WT, C))
        return jnp.concatenate(parts, axis=1)

    def conv(S, w, use):
        def body(i, carry):
            r0 = i * RB
            use(r0, jnp.dot(windows(S, r0, False), w[...].reshape(9 * C, C), preferred_element_type=f32))
            return carry

        lax.fori_loop(0, HT // RB, body, 0)

    def convt(S, w, use):
        def body(i, carry):
            r0 = i * RB
            wide = jnp.concatenate([w[k] for k in range(9)], axis=1)
            use(r0, lax.dot_general(windows(S, r0, True), wide, NT, preferred_element_type=f32))
            return carry

        lax.fori_loop(0, HT // RB, body, 0)

    def wgrad(g, ut, S):
        def body(k, carry):
            dy, dx = k // 3, lax.rem(k, 3)
            win = S[2 - dx, pl.ds(2 - dy, HT)].reshape(POS, C)
            res = jnp.dot(ut[...], win, preferred_element_type=f32)
            at = pl.ds(pl.multiple_of(k * C, C), C)
            grad[g, 0, at, :] = res[:, :128]
            grad[g, 1, at, :] = res[:, 128:]
            return carry

        lax.fori_loop(0, 9, body, 0)

    partner = {"row": row + 1 - 2 * core, "col": col}

    here = (lax.rem(col, 4), (col // 4) * 2 + ylo, zed)

    def along(axis, v):
        if axis == 0:
            return {"row": row, "col": (col // 4) * 4 + v}
        if axis == 1:
            return {"row": lax.rem(v, 2) * 8 + lax.rem(row, 8), "col": (v // 2) * 4 + lax.rem(col, 4)}
        return {"row": ylo * 8 + v * 2 + core, "col": col}

    def others(axis, send):
        def go(j, carry):
            t = lax.rem(here[axis] + j, 4)
            send(t, along(axis, t))
            return carry

        lax.fori_loop(1, 4, go, 0)

    def pair0(g):
        return remote(grad.at[g, 1 - core], p0r.at[g], g_send.at[g, 0], g_recv.at[g, 0], partner)

    def ar0(g):
        pair0(g).start()

    def ar1(g):
        pair0(g).wait()

        def add(j, carry):
            at = pl.ds(pl.multiple_of(j * 192, 64), 192)
            rss[g, j] = grad[g, core, at, :] + p0r[g, at, :]
            return carry

        lax.fori_loop(0, 12, add, 0)
        for t in range(3):
            mine = t * 4 + here[t]
            rsr[g, mine] = rss[g, mine]
            others(
                t,
                lambda v, dev, t=t, mine=mine: remote(
                    rss.at[g, t * 4 + v], rsr.at[g, mine], g_send.at[g, 1], g_recv.at[g, 1], dev
                ).start(),
            )

    def ar2(g):
        drain(rss.at[g, pl.ds(0, 9)], g_send.at[g, 1])
        drain(rsr.at[g, pl.ds(0, 9)], g_recv.at[g, 1])
        for t in range(3):
            for c in range(4):
                at = slice(c * 48, (c + 1) * 48)
                tb[g, t * 4 + c] = (rsr[g, t * 4, at] + rsr[g, t * 4 + 1, at]) + (
                    rsr[g, t * 4 + 2, at] + rsr[g, t * 4 + 3, at]
                )
        for t in range(3):
            a = (t + 1) % 3
            mine = t * 4 + here[a]
            tr[g, mine] = tb[g, mine]
            others(
                a,
                lambda v, dev, t=t, mine=mine: remote(
                    tb.at[g, t * 4 + v], tr.at[g, mine], g_send.at[g, 2], g_recv.at[g, 2], dev
                ).start(),
            )

    def ar3(g):
        drain(tb.at[g, pl.ds(0, 9)], g_send.at[g, 2])
        drain(tr.at[g, pl.ds(0, 9)], g_recv.at[g, 2])
        for t in range(3):
            a = (t + 2) % 3
            mine = zr.at[g, t * 4 + here[a]]
            zr[g, t * 4 + here[a]] = (tr[g, t * 4] + tr[g, t * 4 + 1]) + (tr[g, t * 4 + 2] + tr[g, t * 4 + 3])
            others(
                a,
                lambda v, dev, mine=mine: remote(mine, mine, g_send.at[g, 3], g_recv.at[g, 3], dev).start(),
            )

    def ar4(g):
        drain(zr.at[g, pl.ds(0, 9)], g_send.at[g, 3])
        drain(zr.at[g, pl.ds(0, 9)], g_recv.at[g, 3])
        for t in range(3):
            a = (t + 1) % 3
            at = t * 16 + here[t] * 4 + here[a]
            ag[g, core, at] = ((zr[g, t * 4] + zr[g, t * 4 + 1]) + (zr[g, t * 4 + 2] + zr[g, t * 4 + 3])).astype(bf16)
            mine = ag.at[g, core, at]
            others(
                a,
                lambda v, dev, mine=mine: remote(mine, mine, g_send.at[g, 4], g_recv.at[g, 4], dev).start(),
            )

    def ar5(g):
        drain(ag.at[g, 0, pl.ds(0, 9)], g_send.at[g, 4])
        drain(ag.at[g, 0, pl.ds(0, 9)], g_recv.at[g, 4])
        for t in range(3):
            mine = ag.at[g, core, pl.ds(t * 16 + here[t] * 4, 4)]
            others(
                t,
                lambda v, dev, mine=mine: remote(mine, mine, g_send.at[g, 5], g_recv.at[g, 5], dev).start(),
            )

    def pair6(g):
        mine = ag.at[g, core]
        return remote(mine, mine, g_send.at[g, 6], g_recv.at[g, 6], partner)

    def ar6(g):
        drain(ag.at[g, 0, pl.ds(0, 36)], g_send.at[g, 5])
        drain(ag.at[g, 0, pl.ds(0, 36)], g_recv.at[g, 5])
        pair6(g).start()

    def ar7(g):
        pair6(g).wait()
        for half in range(2):
            wg_out[g, :, half * 128 : (half + 1) * 128] = ag[g, half].reshape(9 * C, 128)

    def sum_send(a):
        stat[a, me] = msg[a]

        def send(j, carry):
            remote(msg.at[a], stat.at[a, me], s_send.at[a], s_recv.at[a], peer(j)[1]).start()
            return carry

        lax.fori_loop(1, N, send, 0)

    def sum_finish(a):
        drain(stat.at[a, pl.ds(0, N - 1)], s_send.at[a])
        drain(stat.at[a, pl.ds(0, N - 1)], s_recv.at[a])
        return jnp.sum(stat[a], axis=0)

    same = (iota((C, C), 0) // (C // G) == iota((C, C), 1) // (C // G)).astype(f32)

    def per_group(v):
        wide = jnp.concatenate([v, jnp.zeros((6, C), f32)], axis=0)
        return jnp.dot(wide, same, precision=lax.Precision.HIGHEST, preferred_element_type=f32)

    parts = cb.shape[0] // STAGE

    def fetch(c, slot):
        return pltpu.make_async_copy(
            cb.at[pl.ds(pl.multiple_of(c * STAGE, STAGE), STAGE)], stage.at[slot], l_sems.at[slot]
        )

    fetch(0, 0).start()
    fetch(1, 1).start()
    cot_copy = pltpu.make_async_copy(cot_hbm, S_a.at[1, pl.ds(1, HT)], l_sems.at[2])
    dec_copy = pltpu.make_async_copy(w_dec_hbm, w_dec, l_sems.at[3])
    enc_copy = pltpu.make_async_copy(w_enc_hbm, w_enc, l_sems.at[4])
    cot_copy.start()
    dec_copy.start()
    enc_copy.start()

    def first(h, carry):
        v = lat[h].astype(f32)
        return carry[0] + jnp.sum(v, 0, keepdims=True), carry[1] + jnp.sum(v * v, 0, keepdims=True)

    zero = jnp.zeros((1, C), f32)
    s1, s2 = lax.fori_loop(0, HT, first, (zero, zero))
    msg[0, 0:1] = s1
    msg[0, 1:2] = s2
    cot_copy.wait()
    field_cols(S_a)
    pl.semaphore_wait(barrier, N - 1)
    sum_send(0)
    halo_send(COT, S_a)

    upper = (iota((WT, WT), 0) < iota((WT, WT), 1)).astype(f32).astype(bf16)
    base = jnp.zeros((N, 1), f32)
    named = jnp.zeros((N, WT), f32)
    for h in range(HT):
        codes = ids_v[h : h + 1, :]
        member = (iota((N, WT), 0) == (codes >> 7)).astype(f32)
        member_b = member.astype(bf16)
        ahead = jnp.dot(member_b, upper, preferred_element_type=f32)
        slot = jnp.sum(member * (ahead + base), axis=0, keepdims=True)
        base = base + jnp.sum(member, axis=1, keepdims=True)
        slots[h : h + 1, :] = slot
        local = ((codes & 127) + 1).astype(f32)
        lanes = (iota((WT, WT), 0) & (CAP - 1)).astype(f32)
        spread = jnp.where(lanes == slot, local, 0.0).astype(bf16)
        named = named + lax.dot_general(member_b, spread, NT, preferred_element_type=f32)
    idrow[:, 0, :] = named - 1.0

    def ids_send(j, carry):
        t, dev = peer(j)
        remote(idrow.at[t], idr.at[me], i_send.at[0], i_recv.at[0], dev).start()
        return carry

    lax.fori_loop(1, N, ids_send, 0)
    idr[me] = idrow[me]

    def convert(c, carry):
        slot = lax.rem(c, 2)
        fetch(c, slot).wait()
        for k in range(STAGE // 128):
            cbf[pl.ds(pl.multiple_of(c * STAGE + k * 128, 128), 128), :] = stage[
                slot, k * 128 : (k + 1) * 128, :
            ].astype(f32)

        @pl.when(c + 2 < parts)
        def _():
            fetch(c + 2, slot).start()

        return carry

    lax.fori_loop(0, parts, convert, 0)

    def pick(h, carry):
        def some(t, inner):
            for j in range(16):
                at = t * 16 + j
                qf[pl.ds(pl.multiple_of(t * 16, 16) + j, 1), :] = cbf[pl.ds(ids_s[h, at], 1), :]
            return inner

        lax.fori_loop(0, WT // 16, some, 0)
        v = qf[...]
        S_q[1, h + 1] = v.astype(bf16)
        qt[:, pl.ds(pl.multiple_of(h * WT, WT), WT)] = v.T.astype(bf16)
        take_cols(h, v)
        return carry

    lax.fori_loop(0, HT, pick, 0)
    halo_send(QNT, S_q)

    tot = sum_finish(0)
    grp = per_group(tot)
    mean = grp[0:1] / count
    var = grp[1:2] / count - mean * mean
    inv = lax.rsqrt(var + epsilon)
    gain_v, bias_v = gain[...], bias[...]

    def smoothing(h, carry):
        act = (lat[h].astype(f32) - mean) * inv * gain_v + bias_v
        v = act * jax.nn.sigmoid(act)
        S_s[1, h + 1] = v.astype(bf16)
        st[:, pl.ds(pl.multiple_of(h * WT, WT), WT)] = v.T.astype(bf16)
        take_cols(h, v)
        return carry

    lax.fori_loop(0, HT, smoothing, 0)
    halo_send(SMO, S_s)

    halo_finish(COT, S_a)
    dec_copy.wait()
    enc_copy.wait()
    wgrad(0, qt, S_a)
    ar0(0)
    convt(S_a, w_dec, lambda r0, v: put(BQ, r0, v))
    ar1(0)
    halo_finish(SMO, S_s)

    def keep_enc(r0, v):
        put(ENC, r0, v + lat[pl.ds(r0, RB)].reshape(RB * WT, C).astype(f32))

    conv(S_s, w_enc, keep_enc)
    ar2(0)

    def keep_dec(r0, v):
        dec_out[pl.ds(r0, RB)] = v.reshape(RB, WT, C).astype(bf16)

    code_scale = float(16384) / (HT * WT * N)

    def rotate(h, carry):
        for k in range(4):
            at = slice(k * 32, (k + 1) * 32)
            there = pl.ds(pl.multiple_of(h * WT + k * 32, 32), 32)
            z, b = cbf[pl.ds(pl.multiple_of(ENC + h * WT + k * 32, 32), 32), :], cbf[there, :]
            e = S_q[1, h + 1, at].astype(f32)
            z_norm = jnp.sqrt(jnp.sum(z * z, -1, keepdims=True) + epsilon)
            e_norm = jnp.sqrt(jnp.sum(e * e, -1, keepdims=True) + epsilon)
            z_unit = z * (1.0 / z_norm)
            e_unit = e * (1.0 / e_norm)
            mirror = z_unit + e_unit
            mirror = mirror * (1.0 / jnp.sqrt(jnp.sum(mirror * mirror, -1, keepdims=True) + epsilon))
            along_mirror = jnp.sum(mirror * b, -1, keepdims=True)
            along_code = jnp.sum(e_unit * b, -1, keepdims=True)
            turned = b - (2.0 * along_mirror) * mirror + (2.0 * along_code) * z_unit
            back = (e_norm / z_norm) * turned + commit_beta * (z - e)
            cbf[pl.ds(pl.multiple_of(EB + h * WT + k * 32, 32), 32), :] = back
            S_a[1, h + 1, at] = back.astype(bf16)
            pull[there, :] = (code_scale * (e - z)).astype(bf16)
            if k == 0:
                colf[0, pl.ds(h, 1)] = back[0:1]
            if k == 3:
                colf[1, pl.ds(h, 1)] = back[31:32]
        return carry

    lax.fori_loop(0, HT, rotate, 0)
    halo_send(BCK, S_a)
    ar3(0)
    halo_finish(QNT, S_q)

    for h in range(HT):
        at = slice(h * WT, (h + 1) * WT)
        dkey[:, at] = jnp.broadcast_to((ids_v[h : h + 1, :] >> 7).astype(f32), (16, WT)).astype(bf16)
        skey[:, at] = jnp.broadcast_to(slots[h : h + 1, :], (16, WT)).astype(bf16)
    low = iota((16, POS), 0).astype(f32).astype(bf16)
    one, nil, gone = jnp.ones((16, POS), bf16), jnp.zeros((16, POS), bf16), jnp.full((16, POS), -1.0, bf16)

    def pack(i, carry):
        first_owner = lax.rem(me // 8 + i, N // 8) * 8
        parts = []
        for j in range(8):
            owner = jnp.full((16, POS), (first_owner + j).astype(f32), f32).astype(bf16)
            key = jnp.where(dkey[...] == owner, skey[...], gone)
            parts.append(jnp.where(key == low, one, nil))
            parts.append(jnp.where(key == low + 16.0, one, nil))
        select = jnp.concatenate(parts, axis=0)
        rows = jnp.dot(select, pull[...], preferred_element_type=f32)
        sb[pl.ds(first_owner, 8)] = rows.reshape(8, CAP, C).astype(bf16)
        return carry

    lax.fori_loop(0, N // 8, pack, 0)

    def rows_send(j, carry):
        t, dev = peer(j)
        remote(sb.at[t], rb.at[me], c_send.at[0], c_recv.at[0], dev).start()
        return carry

    rb[me] = sb[me]
    ar4(0)

    halo_finish(BCK, S_a)
    wgrad(1, st, S_a)
    ar0(1)
    lax.fori_loop(1, 32, rows_send, 0)
    ar5(0)

    def backward(r0, v):
        bs = v.reshape(RB, WT, C)
        s_b, s_g = zero, zero
        for k in range(RB):
            normed = (lat[r0 + k].astype(f32) - mean) * inv
            act = normed * gain_v + bias_v
            s = jax.nn.sigmoid(act)
            t = bs[k] * s * (1.0 + act * (1.0 - s))
            put(BA, r0 + k, t)
            s_b = s_b + jnp.sum(t, 0, keepdims=True)
            s_g = s_g + jnp.sum(t * normed, 0, keepdims=True)
        msg[1, 0:1] += s_b
        msg[1, 1:2] += s_g

    msg[1] = jnp.zeros((2, C), f32)
    convt(S_a, w_enc, backward)
    ar1(1)
    sum_send(1)
    lax.fori_loop(32, 64, rows_send, 0)
    ar6(0)
    conv(S_q, w_dec, keep_dec)
    ar2(1)
    lax.fori_loop(64, 96, rows_send, 0)
    ar7(0)

    tot2 = sum_finish(1)
    gsum_out[...] = tot2
    means = per_group(tot2 * gain_v) * (1.0 / count)
    mean1, mean2 = means[0:1], means[1:2]

    def last(h, carry):
        normed = (lat[h].astype(f32) - mean) * inv
        lg_out[h] = (inv * (row_of(BA, h) * gain_v - mean1 - normed * mean2) + row_of(EB, h)).astype(bf16)
        return carry

    lax.fori_loop(0, HT, last, 0)
    ar3(1)
    lax.fori_loop(96, N, rows_send, 0)
    ar4(1)
    ar5(1)
    ar6(1)

    drain(idr.at[pl.ds(0, N - 1)], i_send.at[0])
    drain(idr.at[pl.ds(0, N - 1)], i_recv.at[0])
    drain(sb.at[pl.ds(0, N - 1)], c_send.at[0])
    drain(rb.at[pl.ds(0, N - 1)], c_recv.at[0])
    quarter = iota((1, WT), 1) // CAP

    def collect(g, acc):
        hot = []
        for half in range(2):
            names = idr[g * 8 + half * 4]
            for j in range(1, 4):
                names = jnp.where(quarter == j, idr[g * 8 + half * 4 + j], names)
            hot.append((iota((N, WT), 0).astype(f32) == names).astype(f32).astype(bf16))
        rows = rb[pl.ds(g * 8, 8)].reshape(8 * CAP, C)
        return acc + jnp.dot(jnp.concatenate(hot, axis=1), rows, preferred_element_type=f32)

    cg_out[...] = lax.fori_loop(0, N // 8, collect, jnp.zeros((N, C), f32))
    ar7(1)


def main(lat, code_ids, gain, bias, w_enc, w_dec, cot, codebook):
    dma = pltpu.SemaphoreType.DMA
    V = pltpu.VMEM
    field = V((3, HT + 2, WT, C), bf16)
    return pl.pallas_call(
        main_kernel,
        out_shape=(
            jax.ShapeDtypeStruct((HT, WT, C), bf16),
            jax.ShapeDtypeStruct((HT, WT, C), bf16),
            jax.ShapeDtypeStruct((2, C), f32),
            jax.ShapeDtypeStruct((2, 9 * C, C), bf16),
            jax.ShapeDtypeStruct((N, C), f32),
        ),
        in_specs=[VM, SM, VM, VM, VM, ANY, ANY, ANY, ANY],
        out_specs=(VM,) * 5,
        scratch_shapes=[
            field, field, field,
            V((4, 2, WT, C), bf16), V((4, 6, HT, C), bf16), V((4, 2, HT, C), bf16),
            V((2, HT, C), f32), V((2, 32, C), f32),
            V((codebook.shape[0], C), f32), V((2, STAGE, C), bf16), V((WT, C), f32), V((HT, WT), f32),
            V((N, 1, WT), f32), V((C, POS), bf16), V((9, C, C), bf16), V((9, C, C), bf16),
            V((POS, C), bf16), V((C, POS), bf16),
            V((2, 2, C), f32), V((2, N, 2, C), f32),
            V((N, CAP, C), bf16), V((N, CAP, C), bf16), V((N, 1, WT), f32),
            V((16, POS), bf16), V((16, POS), bf16),
            V((2, 2, 9 * C, 128), f32), V((2, 9 * C, 128), f32),
            V((2, 12, 192, 128), f32), V((2, 12, 192, 128), f32), V((2, 12, 48, 128), f32), V((2, 12, 48, 128), f32),
            V((2, 12, 48, 128), f32), V((2, 2, 48, 48, 128), bf16),
            dma((5,)), dma((4, 8)), dma((4, 8)), dma((2,)), dma((2,)), dma((1,)), dma((1,)), dma((1,)), dma((1,)),
            dma((2, 7)), dma((2, 7)),
        ],
        compiler_params=pltpu.CompilerParams(
            collective_id=0, has_side_effects=True, vmem_limit_bytes=67_000_000
        ),
        name="main",
    )(lat, code_ids, code_ids, gain, bias, w_enc, w_dec, cot, codebook)


def body(latents, code_ids, norm_gain, norm_bias, encoder_weight, codebook, decoder_weight, cotangent):
    decoded, latents_grad, gsum, wg, cg = main(
        latents, code_ids, norm_gain.reshape(1, C), norm_bias.reshape(1, C),
        encoder_weight.reshape(9, C, C), decoder_weight.reshape(9, C, C), cotangent, codebook,
    )
    wg = wg.reshape(2, 3, 3, C, C).astype(f32)
    return decoded, latents_grad, gsum[1], gsum[0], wg[1], wg[0], cg


def solution(mesh):
    tiled = P("row", "col", None)
    in_specs = (tiled, P("row", "col"), P(), P(), P(), P(), P(), tiled)
    out_specs = (tiled, tiled, P(), P(), P(), P(), P(("row", "col"), None))
    return jax.shard_map(body, mesh=mesh, in_specs=in_specs, out_specs=out_specs, check_vma=False)
```

```python
import functools

import jax
import jax.numpy as jnp
from jax import lax
from jax.experimental import pallas as pl
from jax.experimental.pallas import tpu as pltpu
from jax.sharding import PartitionSpec as P

G = 32
NR, NC = 16, 8
N = NR * NC
HT, WT, C = 16, 128, 256
POS = HT * WT
CAP = 32
epsilon = 1e-06
commit_beta = 0.25
f32, bf16, i32 = jnp.float32, jnp.bfloat16, jnp.int32
MESH = pl.DeviceIdType.MESH
VM = pl.BlockSpec(memory_space=pltpu.VMEM)
SM = pl.BlockSpec(memory_space=pltpu.SMEM)
ANY = pl.BlockSpec(memory_space=pl.ANY)
NT = (((1,), (1,)), ((), ()))


def iota(shape, dim):
    return lax.broadcasted_iota(i32, shape, dim)


COT, QNT, SMO, BCK = 0, 1, 2, 3


def main_kernel(
    lat, ids_s, ids_v, gain, bias, w_enc_hbm, w_dec_hbm, cot_hbm, cb,
    dec_out, lg_out, gsum_out, wg_out, cg_out,
    S_a, S_q, S_s, hr, hc, hs, colf, cf,
    cbf, qf, slots, idrow, qt, w_enc, w_dec, pull, st,
    msg, stat, sb, rb, idr, dkey, skey,
    grad, p0r, rss, rsr, tb, tr, zr, ag,
    l_sems, h_send, h_recv, s_send, s_recv, i_send, i_recv, c_send, c_recv, g_send, g_recv,
):
    row, col = lax.axis_index("row"), lax.axis_index("col")
    me = row * NC + col
    core = lax.rem(row, 2)
    zed = lax.rem(row // 2, 4)
    ylo = row // 8
    up, dn = lax.rem(row + NR - 1, NR), lax.rem(row + 1, NR)
    lf, rt = lax.rem(col + NC - 1, NC), lax.rem(col + 1, NC)
    count = float(HT * WT * N * (C // G))

    barrier = pltpu.get_barrier_semaphore()

    def peer(j):
        t = lax.rem(me + j, N)
        return t, {"row": t // NC, "col": lax.rem(t, NC)}

    def hello(j, carry):
        pl.semaphore_signal(barrier, inc=1, device_id=peer(j)[1], device_id_type=MESH)
        return carry

    lax.fori_loop(1, N, hello, 0)

    def remote(src, dst, ss, rs, dev):
        return pltpu.make_async_remote_copy(
            src_ref=src, dst_ref=dst, send_sem=ss, recv_sem=rs, device_id=dev, device_id_type=MESH
        )

    def drain(ref, sem):
        pltpu.make_async_copy(ref, ref, sem).wait()

    def halo_copies(f, S):
        here = {
            0: (S.at[1, HT], hr.at[f, 0], dn, col),
            1: (S.at[1, 1], hr.at[f, 1], up, col),
            2: (hs.at[f, 1], hc.at[f, 1], row, rt),
            3: (hs.at[f, 1], hc.at[f, 0], dn, rt),
            4: (hs.at[f, 1], hc.at[f, 2], up, rt),
            5: (hs.at[f, 0], hc.at[f, 4], row, lf),
            6: (hs.at[f, 0], hc.at[f, 3], dn, lf),
            7: (hs.at[f, 0], hc.at[f, 5], up, lf),
        }
        return [
            remote(s, d, h_send.at[f, k], h_recv.at[f, k], {"row": r, "col": c})
            for k, (s, d, r, c) in here.items()
        ]

    def halo_send(f, S):
        hs[f] = colf[...].astype(bf16)
        for copy in halo_copies(f, S):
            copy.start()

    ok_u = jnp.where(row > 0, 1.0, 0.0).astype(f32)
    ok_d = jnp.where(row < NR - 1, 1.0, 0.0).astype(f32)
    ok_l = jnp.where(col > 0, 1.0, 0.0).astype(f32)
    ok_r = jnp.where(col < NC - 1, 1.0, 0.0).astype(f32)

    def halo_finish(f, S):
        for copy in halo_copies(f, S):
            copy.wait()
        S[1, 0] = (hr[f, 0].astype(f32) * ok_u).astype(bf16)
        S[1, HT + 1] = (hr[f, 1].astype(f32) * ok_d).astype(bf16)
        for side, ok in ((0, ok_l), (1, ok_r)):
            above = hc[f, 3 * side].astype(f32) * (ok * ok_u)
            below = hc[f, 3 * side + 2].astype(f32) * (ok * ok_d)
            cf[side, 8:24] = hc[f, 3 * side + 1].astype(f32) * ok
            cf[side, 7:8] = above[15:16]
            cf[side, 24:25] = below[0:1]

        def shift(hh, carry):
            v = S[1, hh].astype(f32)
            place = iota((WT, C), 0)
            S[0, hh] = jnp.where(place == 0, cf[0, pl.ds(hh + 7, 1)], pltpu.roll(v, 1, 0)).astype(bf16)
            S[2, hh] = jnp.where(
                place == WT - 1, cf[1, pl.ds(hh + 7, 1)], pltpu.roll(v, WT - 1, 0)
            ).astype(bf16)
            return carry

        lax.fori_loop(0, HT + 2, shift, 0)

    def take_cols(h, v):
        colf[0, pl.ds(h, 1)] = v[0:1]
        colf[1, pl.ds(h, 1)] = v[WT - 1 : WT]

    def field_cols(S):
        def body(h, carry):
            take_cols(h, S[1, h + 1].astype(f32))
            return carry

        lax.fori_loop(0, HT, body, 0)

    BQ, ENC, EB, BA = 0, POS, 2 * POS, 3 * POS

    def put(plane, r0, v):
        cbf[pl.ds(pl.multiple_of(plane + r0 * WT, WT), v.shape[0]), :] = v

    def row_of(plane, h):
        return cbf[pl.ds(pl.multiple_of(plane + h * WT, WT), WT), :]

    RB = 4

    def windows(S, r0, flip):
        parts = []
        for dy in range(3):
            for dx in range(3):
                a, b = (2 - dx, 2 - dy) if flip else (dx, dy)
                parts.append(S[a, pl.ds(r0 + b, RB)].reshape(RB * WT, C))
        return jnp.concatenate(parts, axis=1)

    def conv(S, w, use):
        def body(i, carry):
            r0 = i * RB
            use(r0, jnp.dot(windows(S, r0, False), w[...].reshape(9 * C, C), preferred_element_type=f32))
            return carry

        lax.fori_loop(0, HT // RB, body, 0)

    def convt(S, w, use):
        def body(i, carry):
            r0 = i * RB
            wide = jnp.concatenate([w[k] for k in range(9)], axis=1)
            use(r0, lax.dot_general(windows(S, r0, True), wide, NT, preferred_element_type=f32))
            return carry

        lax.fori_loop(0, HT // RB, body, 0)

    def wgrad(g, ut, S):
        def body(k, carry):
            dy, dx = k // 3, lax.rem(k, 3)
            win = S[2 - dx, pl.ds(2 - dy, HT)].reshape(POS, C)
            res = jnp.dot(ut[...], win, preferred_element_type=f32)
            at = pl.ds(pl.multiple_of(k * C, C), C)
            grad[g, 0, at, :] = res[:, :128]
            grad[g, 1, at, :] = res[:, 128:]
            return carry

        lax.fori_loop(0, 9, body, 0)

    partner = {"row": row + 1 - 2 * core, "col": col}

    here = (lax.rem(col, 4), (col // 4) * 2 + ylo, zed)

    def along(axis, v):
        if axis == 0:
            return {"row": row, "col": (col // 4) * 4 + v}
        if axis == 1:
            return {"row": lax.rem(v, 2) * 8 + lax.rem(row, 8), "col": (v // 2) * 4 + lax.rem(col, 4)}
        return {"row": ylo * 8 + v * 2 + core, "col": col}

    def others(axis, send):
        def go(j, carry):
            t = lax.rem(here[axis] + j, 4)
            send(t, along(axis, t))
            return carry

        lax.fori_loop(1, 4, go, 0)

    def pair0(g):
        return remote(grad.at[g, 1 - core], p0r.at[g], g_send.at[g, 0], g_recv.at[g, 0], partner)

    def ar0(g):
        pair0(g).start()

    def ar1(g):
        pair0(g).wait()

        def add(j, carry):
            at = pl.ds(pl.multiple_of(j * 192, 64), 192)
            rss[g, j] = grad[g, core, at, :] + p0r[g, at, :]
            return carry

        lax.fori_loop(0, 12, add, 0)
        for t in range(3):
            mine = t * 4 + here[t]
            rsr[g, mine] = rss[g, mine]
            others(
                t,
                lambda v, dev, t=t, mine=mine: remote(
                    rss.at[g, t * 4 + v], rsr.at[g, mine], g_send.at[g, 1], g_recv.at[g, 1], dev
                ).start(),
            )

    def ar2(g):
        drain(rss.at[g, pl.ds(0, 9)], g_send.at[g, 1])
        drain(rsr.at[g, pl.ds(0, 9)], g_recv.at[g, 1])
        for t in range(3):
            for c in range(4):
                at = slice(c * 48, (c + 1) * 48)
                tb[g, t * 4 + c] = (rsr[g, t * 4, at] + rsr[g, t * 4 + 1, at]) + (
                    rsr[g, t * 4 + 2, at] + rsr[g, t * 4 + 3, at]
                )
        for t in range(3):
            a = (t + 1) % 3
            mine = t * 4 + here[a]
            tr[g, mine] = tb[g, mine]
            others(
                a,
                lambda v, dev, t=t, mine=mine: remote(
                    tb.at[g, t * 4 + v], tr.at[g, mine], g_send.at[g, 2], g_recv.at[g, 2], dev
                ).start(),
            )

    def ar3(g):
        drain(tb.at[g, pl.ds(0, 9)], g_send.at[g, 2])
        drain(tr.at[g, pl.ds(0, 9)], g_recv.at[g, 2])
        for t in range(3):
            a = (t + 2) % 3
            mine = zr.at[g, t * 4 + here[a]]
            zr[g, t * 4 + here[a]] = (tr[g, t * 4] + tr[g, t * 4 + 1]) + (tr[g, t * 4 + 2] + tr[g, t * 4 + 3])
            others(
                a,
                lambda v, dev, mine=mine: remote(mine, mine, g_send.at[g, 3], g_recv.at[g, 3], dev).start(),
            )

    def ar4(g):
        drain(zr.at[g, pl.ds(0, 9)], g_send.at[g, 3])
        drain(zr.at[g, pl.ds(0, 9)], g_recv.at[g, 3])
        for t in range(3):
            a = (t + 1) % 3
            at = t * 16 + here[t] * 4 + here[a]
            ag[g, core, at] = ((zr[g, t * 4] + zr[g, t * 4 + 1]) + (zr[g, t * 4 + 2] + zr[g, t * 4 + 3])).astype(bf16)
            mine = ag.at[g, core, at]
            others(
                a,
                lambda v, dev, mine=mine: remote(mine, mine, g_send.at[g, 4], g_recv.at[g, 4], dev).start(),
            )

    def ar5(g):
        drain(ag.at[g, 0, pl.ds(0, 9)], g_send.at[g, 4])
        drain(ag.at[g, 0, pl.ds(0, 9)], g_recv.at[g, 4])
        for t in range(3):
            mine = ag.at[g, core, pl.ds(t * 16 + here[t] * 4, 4)]
            others(
                t,
                lambda v, dev, mine=mine: remote(mine, mine, g_send.at[g, 5], g_recv.at[g, 5], dev).start(),
            )

    def pair6(g):
        mine = ag.at[g, core]
        return remote(mine, mine, g_send.at[g, 6], g_recv.at[g, 6], partner)

    def ar6(g):
        drain(ag.at[g, 0, pl.ds(0, 36)], g_send.at[g, 5])
        drain(ag.at[g, 0, pl.ds(0, 36)], g_recv.at[g, 5])
        pair6(g).start()

    def ar7(g):
        pair6(g).wait()
        for half in range(2):
            wg_out[g, :, half * 128 : (half + 1) * 128] = ag[g, half].reshape(9 * C, 128)

    def sum_send(a):
        stat[a, me] = msg[a]

        def send(j, carry):
            remote(msg.at[a], stat.at[a, me], s_send.at[a], s_recv.at[a], peer(j)[1]).start()
            return carry

        lax.fori_loop(1, N, send, 0)

    def sum_finish(a):
        drain(stat.at[a, pl.ds(0, N - 1)], s_send.at[a])
        drain(stat.at[a, pl.ds(0, N - 1)], s_recv.at[a])
        return jnp.sum(stat[a], axis=0)

    same = (iota((C, C), 0) // (C // G) == iota((C, C), 1) // (C // G)).astype(f32)

    def per_group(v):
        wide = jnp.concatenate([v, jnp.zeros((6, C), f32)], axis=0)
        return jnp.dot(wide, same, precision=lax.Precision.HIGHEST, preferred_element_type=f32)

    parts = cb.shape[0] // HT
    slots_of = [(S_s, 0), (S_s, 1), (S_s, 2), (S_q, 0), (S_q, 1), (S_q, 2)]

    def slot_of(c):
        S, k = slots_of[c % 6]
        return S.at[k, pl.ds(0, HT)]

    def fetch(c):
        return pltpu.make_async_copy(cb.at[pl.ds(c * HT, HT)], slot_of(c), l_sems.at[c % 6])

    cot_copy = pltpu.make_async_copy(cot_hbm, S_a.at[1, pl.ds(1, HT)], l_sems.at[6])
    dec_copy = pltpu.make_async_copy(w_dec_hbm, w_dec, l_sems.at[7])
    enc_copy = pltpu.make_async_copy(w_enc_hbm, w_enc, l_sems.at[8])
    cot_copy.start()
    for c in range(6):
        fetch(c).start()
    dec_copy.start()
    enc_copy.start()

    def first(h, carry):
        v = lat[h].astype(f32)
        return carry[0] + jnp.sum(v, 0, keepdims=True), carry[1] + jnp.sum(v * v, 0, keepdims=True)

    zero = jnp.zeros((1, C), f32)
    s1, s2 = lax.fori_loop(0, HT, first, (zero, zero))
    msg[0, 0:1] = s1
    msg[0, 1:2] = s2
    cot_copy.wait()
    field_cols(S_a)
    pl.semaphore_wait(barrier, N - 1)
    sum_send(0)
    halo_send(COT, S_a)

    upper = (iota((WT, WT), 0) < iota((WT, WT), 1)).astype(f32).astype(bf16)
    base = jnp.zeros((N, 1), f32)
    named = jnp.zeros((N, WT), f32)
    for h in range(HT):
        codes = ids_v[h : h + 1, :]
        member = (iota((N, WT), 0) == (codes >> 7)).astype(f32)
        member_b = member.astype(bf16)
        ahead = jnp.dot(member_b, upper, preferred_element_type=f32)
        slot = jnp.sum(member * (ahead + base), axis=0, keepdims=True)
        base = base + jnp.sum(member, axis=1, keepdims=True)
        slots[h : h + 1, :] = slot
        local = ((codes & 127) + 1).astype(f32)
        lanes = (iota((WT, WT), 0) & (CAP - 1)).astype(f32)
        spread = jnp.where(lanes == slot, local, 0.0).astype(bf16)
        named = named + lax.dot_general(member_b, spread, NT, preferred_element_type=f32)
    idrow[:, 0, :] = named - 1.0

    def ids_send(j, carry):
        t, dev = peer(j)
        remote(idrow.at[t], idr.at[me], i_send.at[0], i_recv.at[0], dev).start()
        return carry

    lax.fori_loop(1, N, ids_send, 0)
    idr[me] = idrow[me]

    for c in range(parts):
        fetch(c).wait()
        S, k = slots_of[c % 6]

        def convert(h, carry, c=c, S=S, k=k):
            cbf[pl.ds(pl.multiple_of((c * HT + h) * WT, WT), WT), :] = S[k, h].astype(f32)
            return carry

        lax.fori_loop(0, HT, convert, 0)
        if c + 6 < parts:
            fetch(c + 6).start()

    def pick(h, carry):
        def some(t, inner):
            for j in range(16):
                at = t * 16 + j
                qf[pl.ds(pl.multiple_of(t * 16, 16) + j, 1), :] = cbf[pl.ds(ids_s[h * WT + at], 1), :]
            return inner

        lax.fori_loop(0, WT // 16, some, 0)
        v = qf[...]
        S_q[1, h + 1] = v.astype(bf16)
        qt[:, pl.ds(pl.multiple_of(h * WT, WT), WT)] = v.T.astype(bf16)
        take_cols(h, v)
        return carry

    lax.fori_loop(0, HT, pick, 0)
    halo_send(QNT, S_q)

    tot = sum_finish(0)
    grp = per_group(tot)
    mean = grp[0:1] / count
    var = grp[1:2] / count - mean * mean
    inv = lax.rsqrt(var + epsilon)
    gain_v, bias_v = gain[...], bias[...]

    def smoothing(h, carry):
        act = (lat[h].astype(f32) - mean) * inv * gain_v + bias_v
        v = act * jax.nn.sigmoid(act)
        S_s[1, h + 1] = v.astype(bf16)
        st[:, pl.ds(pl.multiple_of(h * WT, WT), WT)] = v.T.astype(bf16)
        take_cols(h, v)
        return carry

    lax.fori_loop(0, HT, smoothing, 0)
    halo_send(SMO, S_s)

    halo_finish(COT, S_a)
    dec_copy.wait()
    enc_copy.wait()
    wgrad(0, qt, S_a)
    ar0(0)
    convt(S_a, w_dec, lambda r0, v: put(BQ, r0, v))
    ar1(0)
    halo_finish(SMO, S_s)

    def keep_enc(r0, v):
        put(ENC, r0, v + lat[pl.ds(r0, RB)].reshape(RB * WT, C).astype(f32))

    conv(S_s, w_enc, keep_enc)
    ar2(0)

    def keep_dec(r0, v):
        dec_out[pl.ds(r0, RB)] = v.reshape(RB, WT, C).astype(bf16)

    code_scale = float(16384) / (HT * WT * N)

    def rotate(h, carry):
        for k in range(4):
            at = slice(k * 32, (k + 1) * 32)
            there = pl.ds(pl.multiple_of(h * WT + k * 32, 32), 32)
            z, b = cbf[pl.ds(pl.multiple_of(ENC + h * WT + k * 32, 32), 32), :], cbf[there, :]
            e = S_q[1, h + 1, at].astype(f32)
            z_norm = jnp.sqrt(jnp.sum(z * z, -1, keepdims=True) + epsilon)
            e_norm = jnp.sqrt(jnp.sum(e * e, -1, keepdims=True) + epsilon)
            z_unit = z * (1.0 / z_norm)
            e_unit = e * (1.0 / e_norm)
            mirror = z_unit + e_unit
            mirror = mirror * (1.0 / jnp.sqrt(jnp.sum(mirror * mirror, -1, keepdims=True) + epsilon))
            along_mirror = jnp.sum(mirror * b, -1, keepdims=True)
            along_code = jnp.sum(e_unit * b, -1, keepdims=True)
            turned = b - (2.0 * along_mirror) * mirror + (2.0 * along_code) * z_unit
            back = (e_norm / z_norm) * turned + commit_beta * (z - e)
            cbf[pl.ds(pl.multiple_of(EB + h * WT + k * 32, 32), 32), :] = back
            S_a[1, h + 1, at] = back.astype(bf16)
            pull[there, :] = (code_scale * (e - z)).astype(bf16)
            if k == 0:
                colf[0, pl.ds(h, 1)] = back[0:1]
            if k == 3:
                colf[1, pl.ds(h, 1)] = back[31:32]
        return carry

    lax.fori_loop(0, HT, rotate, 0)
    halo_send(BCK, S_a)
    ar3(0)
    halo_finish(QNT, S_q)

    for h in range(HT):
        at = slice(h * WT, (h + 1) * WT)
        dkey[:, at] = jnp.broadcast_to((ids_v[h : h + 1, :] >> 7).astype(f32), (16, WT)).astype(bf16)
        skey[:, at] = jnp.broadcast_to(slots[h : h + 1, :], (16, WT)).astype(bf16)
    low = iota((16, POS), 0).astype(f32).astype(bf16)
    one, nil, gone = jnp.ones((16, POS), bf16), jnp.zeros((16, POS), bf16), jnp.full((16, POS), -1.0, bf16)

    def pack(i, carry):
        first_owner = lax.rem(me // 8 + i, N // 8) * 8
        parts = []
        for j in range(8):
            owner = jnp.full((16, POS), (first_owner + j).astype(f32), f32).astype(bf16)
            key = jnp.where(dkey[...] == owner, skey[...], gone)
            parts.append(jnp.where(key == low, one, nil))
            parts.append(jnp.where(key == low + 16.0, one, nil))
        select = jnp.concatenate(parts, axis=0)
        rows = jnp.dot(select, pull[...], preferred_element_type=f32)
        sb[pl.ds(first_owner, 8)] = rows.reshape(8, CAP, C).astype(bf16)
        return carry

    def send_block(i):
        first_owner = lax.rem(me // 8 + i, N // 8) * 8

        def go(j, carry):
            t = first_owner + j

            @pl.when(t != me)
            def _():
                dev = {"row": t // NC, "col": lax.rem(t, NC)}
                remote(sb.at[t], rb.at[me], c_send.at[0], c_recv.at[0], dev).start()

            return carry

        lax.fori_loop(0, 8, go, 0)

    def send_blocks(a, b):
        def go(i, carry):
            send_block(i)
            return carry

        lax.fori_loop(a, b, go, 0)

    def pack_send(i, carry):
        pack(i, carry)
        send_block(i)
        return carry

    lax.fori_loop(0, 7, pack_send, 0)
    lax.fori_loop(7, N // 8, pack, 0)

    rb[me] = sb[me]
    ar4(0)

    halo_finish(BCK, S_a)
    wgrad(1, st, S_a)
    ar0(1)
    ar5(0)

    def backward(r0, v):
        bs = v.reshape(RB, WT, C)
        s_b, s_g = zero, zero
        for k in range(RB):
            normed = (lat[r0 + k].astype(f32) - mean) * inv
            act = normed * gain_v + bias_v
            s = jax.nn.sigmoid(act)
            t = bs[k] * s * (1.0 + act * (1.0 - s))
            put(BA, r0 + k, t)
            s_b = s_b + jnp.sum(t, 0, keepdims=True)
            s_g = s_g + jnp.sum(t * normed, 0, keepdims=True)
        msg[1, 0:1] += s_b
        msg[1, 1:2] += s_g

    msg[1] = jnp.zeros((2, C), f32)
    convt(S_a, w_enc, backward)
    ar1(1)
    sum_send(1)
    send_blocks(7, 10)
    ar6(0)
    conv(S_q, w_dec, keep_dec)
    ar2(1)
    send_blocks(10, 13)
    ar7(0)

    tot2 = sum_finish(1)
    gsum_out[...] = tot2
    means = per_group(tot2 * gain_v) * (1.0 / count)
    mean1, mean2 = means[0:1], means[1:2]

    def last(h, carry):
        normed = (lat[h].astype(f32) - mean) * inv
        lg_out[h] = (inv * (row_of(BA, h) * gain_v - mean1 - normed * mean2) + row_of(EB, h)).astype(bf16)
        return carry

    lax.fori_loop(0, HT, last, 0)
    ar3(1)
    send_blocks(13, 16)
    ar4(1)
    ar5(1)
    ar6(1)

    drain(idr.at[pl.ds(0, N - 1)], i_send.at[0])
    drain(idr.at[pl.ds(0, N - 1)], i_recv.at[0])
    drain(sb.at[pl.ds(0, N - 1)], c_send.at[0])
    drain(rb.at[pl.ds(0, N - 1)], c_recv.at[0])
    quarter = iota((1, WT), 1) // CAP

    def collect(g, acc):
        hot = []
        for half in range(2):
            names = idr[g * 8 + half * 4]
            for j in range(1, 4):
                names = jnp.where(quarter == j, idr[g * 8 + half * 4 + j], names)
            hot.append((iota((N, WT), 0).astype(f32) == names).astype(f32).astype(bf16))
        rows = rb[pl.ds(g * 8, 8)].reshape(8 * CAP, C)
        return acc + jnp.dot(jnp.concatenate(hot, axis=1), rows, preferred_element_type=f32)

    cg_out[...] = lax.fori_loop(0, N // 8, collect, jnp.zeros((N, C), f32))
    ar7(1)


def main(lat, code_ids, gain, bias, w_enc, w_dec, cot, codebook):
    dma = pltpu.SemaphoreType.DMA
    V = pltpu.VMEM
    field = V((3, HT + 2, WT, C), bf16)
    return pl.pallas_call(
        main_kernel,
        out_shape=(
            jax.ShapeDtypeStruct((HT, WT, C), bf16),
            jax.ShapeDtypeStruct((HT, WT, C), bf16),
            jax.ShapeDtypeStruct((2, C), f32),
            jax.ShapeDtypeStruct((2, 9 * C, C), bf16),
            jax.ShapeDtypeStruct((N, C), f32),
        ),
        in_specs=[VM, SM, VM, VM, VM, ANY, ANY, ANY, ANY],
        out_specs=(VM,) * 5,
        scratch_shapes=[
            field, field, field,
            V((4, 2, WT, C), bf16), V((4, 6, HT, C), bf16), V((4, 2, HT, C), bf16),
            V((2, HT, C), f32), V((2, 32, C), f32),
            V((codebook.shape[0] * WT, C), f32), V((WT, C), f32), V((HT, WT), f32),
            V((N, 1, WT), f32), V((C, POS), bf16), V((9, C, C), bf16), V((9, C, C), bf16),
            V((POS, C), bf16), V((C, POS), bf16),
            V((2, 2, C), f32), V((2, N, 2, C), f32),
            V((N, CAP, C), bf16), V((N, CAP, C), bf16), V((N, 1, WT), f32),
            V((16, POS), bf16), V((16, POS), bf16),
            V((2, 2, 9 * C, 128), f32), V((2, 9 * C, 128), f32),
            V((2, 12, 192, 128), f32), V((2, 12, 192, 128), f32), V((2, 12, 48, 128), f32), V((2, 12, 48, 128), f32),
            V((2, 12, 48, 128), f32), V((2, 2, 48, 48, 128), bf16),
            dma((9,)), dma((4, 8)), dma((4, 8)), dma((2,)), dma((2,)), dma((1,)), dma((1,)), dma((1,)), dma((1,)),
            dma((2, 7)), dma((2, 7)),
        ],
        compiler_params=pltpu.CompilerParams(
            collective_id=0, has_side_effects=True, vmem_limit_bytes=67_000_000
        ),
        name="main",
    )(lat, code_ids.reshape(POS), code_ids, gain, bias, w_enc, w_dec, cot, codebook)


def body(latents, code_ids, norm_gain, norm_bias, encoder_weight, codebook, decoder_weight, cotangent):
    decoded, latents_grad, gsum, wg, cg = main(
        latents, code_ids, norm_gain.reshape(1, C), norm_bias.reshape(1, C),
        encoder_weight.reshape(9, C, C), decoder_weight.reshape(9, C, C), cotangent, codebook.reshape(-1, WT, C),
    )
    wg = wg.reshape(2, 3, 3, C, C).astype(f32)
    return decoded, latents_grad, gsum[1], gsum[0], wg[1], wg[0], cg


def solution(mesh):
    tiled = P("row", "col", None)
    in_specs = (tiled, P("row", "col"), P(), P(), P(), P(), P(), tiled)
    out_specs = (tiled, tiled, P(), P(), P(), P(), P(("row", "col"), None))
    return jax.shard_map(body, mesh=mesh, in_specs=in_specs, out_specs=out_specs, check_vma=False)
```

```python
import functools

import jax
import jax.numpy as jnp
from jax import lax
from jax.experimental import pallas as pl
from jax.experimental.pallas import tpu as pltpu
from jax.sharding import PartitionSpec as P

G = 32
NR, NC = 16, 8
N = NR * NC
HT, WT, C = 16, 128, 256
POS = HT * WT
CAP = 32
epsilon = 1e-06
commit_beta = 0.25
f32, bf16, i32 = jnp.float32, jnp.bfloat16, jnp.int32
MESH = pl.DeviceIdType.MESH
VM = pl.BlockSpec(memory_space=pltpu.VMEM)
SM = pl.BlockSpec(memory_space=pltpu.SMEM)
ANY = pl.BlockSpec(memory_space=pl.ANY)
NT = (((1,), (1,)), ((), ()))


def iota(shape, dim):
    return lax.broadcasted_iota(i32, shape, dim)


COT, QNT, SMO, BCK = 0, 1, 2, 3


def main_kernel(
    lat, ids_s, ids_v, gain, bias, w_enc_hbm, w_dec_hbm, cot_hbm, cb,
    dec_out, lg_out, gsum_out, wg_out, cg_out,
    S_a, S_q, S_s, hr, hc, hs, colf, cf,
    cbf, qf, slots, idrow, qt, w_enc, w_dec, pull, st,
    msg, stat, sb, rb, idr, dkey, skey,
    grad, p0r, rss, rsr, tb, tr, zr, ag,
    l_sems, h_send, h_recv, s_send, s_recv, i_send, i_recv, c_send, c_recv, p_send, p_recv, g_send, g_recv,
):
    row, col = lax.axis_index("row"), lax.axis_index("col")
    me = row * NC + col
    core = lax.rem(row, 2)
    zed = lax.rem(row // 2, 4)
    ylo = row // 8
    up, dn = lax.rem(row + NR - 1, NR), lax.rem(row + 1, NR)
    lf, rt = lax.rem(col + NC - 1, NC), lax.rem(col + 1, NC)
    count = float(HT * WT * N * (C // G))

    barrier = pltpu.get_barrier_semaphore()

    def peer(j):
        t = lax.rem(me + j, N)
        return t, {"row": t // NC, "col": lax.rem(t, NC)}

    def hello(j, carry):
        pl.semaphore_signal(barrier, inc=1, device_id=peer(j)[1], device_id_type=MESH)
        return carry

    lax.fori_loop(1, N, hello, 0)

    def remote(src, dst, ss, rs, dev):
        return pltpu.make_async_remote_copy(
            src_ref=src, dst_ref=dst, send_sem=ss, recv_sem=rs, device_id=dev, device_id_type=MESH
        )

    def drain(ref, sem):
        pltpu.make_async_copy(ref, ref, sem).wait()

    def halo_copies(f, S):
        here = {
            0: (S.at[1, HT], hr.at[f, 0], dn, col),
            1: (S.at[1, 1], hr.at[f, 1], up, col),
            2: (hs.at[f, 1], hc.at[f, 1], row, rt),
            3: (hs.at[f, 1], hc.at[f, 0], dn, rt),
            4: (hs.at[f, 1], hc.at[f, 2], up, rt),
            5: (hs.at[f, 0], hc.at[f, 4], row, lf),
            6: (hs.at[f, 0], hc.at[f, 3], dn, lf),
            7: (hs.at[f, 0], hc.at[f, 5], up, lf),
        }
        return [
            remote(s, d, h_send.at[f, k], h_recv.at[f, k], {"row": r, "col": c})
            for k, (s, d, r, c) in here.items()
        ]

    def halo_send(f, S):
        hs[f] = colf[...].astype(bf16)
        for copy in halo_copies(f, S):
            copy.start()

    ok_u = jnp.where(row > 0, 1.0, 0.0).astype(f32)
    ok_d = jnp.where(row < NR - 1, 1.0, 0.0).astype(f32)
    ok_l = jnp.where(col > 0, 1.0, 0.0).astype(f32)
    ok_r = jnp.where(col < NC - 1, 1.0, 0.0).astype(f32)

    def halo_finish(f, S):
        for copy in halo_copies(f, S):
            copy.wait()
        S[1, 0] = (hr[f, 0].astype(f32) * ok_u).astype(bf16)
        S[1, HT + 1] = (hr[f, 1].astype(f32) * ok_d).astype(bf16)
        for side, ok in ((0, ok_l), (1, ok_r)):
            above = hc[f, 3 * side].astype(f32) * (ok * ok_u)
            below = hc[f, 3 * side + 2].astype(f32) * (ok * ok_d)
            cf[side, 8:24] = hc[f, 3 * side + 1].astype(f32) * ok
            cf[side, 7:8] = above[15:16]
            cf[side, 24:25] = below[0:1]

        def shift(hh, carry):
            v = S[1, hh].astype(f32)
            place = iota((WT, C), 0)
            S[0, hh] = jnp.where(place == 0, cf[0, pl.ds(hh + 7, 1)], pltpu.roll(v, 1, 0)).astype(bf16)
            S[2, hh] = jnp.where(
                place == WT - 1, cf[1, pl.ds(hh + 7, 1)], pltpu.roll(v, WT - 1, 0)
            ).astype(bf16)
            return carry

        lax.fori_loop(0, HT + 2, shift, 0)

    def take_cols(h, v):
        colf[0, pl.ds(h, 1)] = v[0:1]
        colf[1, pl.ds(h, 1)] = v[WT - 1 : WT]

    def field_cols(S):
        def body(h, carry):
            take_cols(h, S[1, h + 1].astype(f32))
            return carry

        lax.fori_loop(0, HT, body, 0)

    BQ, ENC, EB, BA = 0, POS, 2 * POS, 3 * POS

    def put(plane, r0, v):
        cbf[pl.ds(pl.multiple_of(plane + r0 * WT, WT), v.shape[0]), :] = v

    def row_of(plane, h):
        return cbf[pl.ds(pl.multiple_of(plane + h * WT, WT), WT), :]

    RB = 4

    def windows(S, r0, flip):
        parts = []
        for dy in range(3):
            for dx in range(3):
                a, b = (2 - dx, 2 - dy) if flip else (dx, dy)
                parts.append(S[a, pl.ds(r0 + b, RB)].reshape(RB * WT, C))
        return jnp.concatenate(parts, axis=1)

    def conv(S, w, use):
        def body(i, carry):
            r0 = i * RB
            use(r0, jnp.dot(windows(S, r0, False), w[...].reshape(9 * C, C), preferred_element_type=f32))
            return carry

        lax.fori_loop(0, HT // RB, body, 0)

    def convt(S, w, use):
        def body(i, carry):
            r0 = i * RB
            wide = jnp.concatenate([w[k] for k in range(9)], axis=1)
            use(r0, lax.dot_general(windows(S, r0, True), wide, NT, preferred_element_type=f32))
            return carry

        lax.fori_loop(0, HT // RB, body, 0)

    partner = {"row": row + 1 - 2 * core, "col": col}

    here = (lax.rem(col, 4), (col // 4) * 2 + ylo, zed)

    def along(axis, v):
        if axis == 0:
            return {"row": row, "col": (col // 4) * 4 + v}
        if axis == 1:
            return {"row": lax.rem(v, 2) * 8 + lax.rem(row, 8), "col": (v // 2) * 4 + lax.rem(col, 4)}
        return {"row": ylo * 8 + v * 2 + core, "col": col}

    def others(axis, send):
        def go(j, carry):
            t = lax.rem(here[axis] + j, 4)
            send(t, along(axis, t))
            return carry

        lax.fori_loop(1, 4, go, 0)

    def pair0(g, t):
        at = pl.ds(t * 768, 768)
        return remote(grad.at[g, 1 - core, at], p0r.at[g, at], p_send.at[g, t], p_recv.at[g, t], partner)

    def wgrad(g, ut, S):
        for dy in range(3):

            def body(dx, carry, dy=dy):
                win = S[2 - dx, 2 - dy : 2 - dy + HT].reshape(POS, C)
                res = jnp.dot(ut[...], win, preferred_element_type=f32)
                at = pl.ds(pl.multiple_of((dy * 3 + dx) * C, C), C)
                grad[g, 0, at, :] = res[:, :128]
                grad[g, 1, at, :] = res[:, 128:]
                return carry

            lax.fori_loop(0, 3, body, 0)
            pair0(g, dy).start()

    def ar1(g):
        for t in range(3):
            pair0(g, t).wait()

            def add(j, carry, t=t):
                at = pl.ds(pl.multiple_of((t * 4 + j) * 192, 64), 192)
                rss[g, t * 4 + j] = grad[g, core, at, :] + p0r[g, at, :]
                return carry

            lax.fori_loop(0, 4, add, 0)
            mine = t * 4 + here[t]
            rsr[g, mine] = rss[g, mine]
            others(
                t,
                lambda v, dev, t=t, mine=mine: remote(
                    rss.at[g, t * 4 + v], rsr.at[g, mine], g_send.at[g, 1], g_recv.at[g, 1], dev
                ).start(),
            )

    def ar2(g):
        drain(rss.at[g, pl.ds(0, 9)], g_send.at[g, 1])
        drain(rsr.at[g, pl.ds(0, 9)], g_recv.at[g, 1])
        for t in range(3):
            for c in range(4):
                at = slice(c * 48, (c + 1) * 48)
                tb[g, t * 4 + c] = (rsr[g, t * 4, at] + rsr[g, t * 4 + 1, at]) + (
                    rsr[g, t * 4 + 2, at] + rsr[g, t * 4 + 3, at]
                )
        for t in range(3):
            a = (t + 1) % 3
            mine = t * 4 + here[a]
            tr[g, mine] = tb[g, mine]
            others(
                a,
                lambda v, dev, t=t, mine=mine: remote(
                    tb.at[g, t * 4 + v], tr.at[g, mine], g_send.at[g, 2], g_recv.at[g, 2], dev
                ).start(),
            )

    def ar3(g):
        drain(tb.at[g, pl.ds(0, 9)], g_send.at[g, 2])
        drain(tr.at[g, pl.ds(0, 9)], g_recv.at[g, 2])
        for t in range(3):
            a = (t + 2) % 3
            mine = zr.at[g, t * 4 + here[a]]
            zr[g, t * 4 + here[a]] = (tr[g, t * 4] + tr[g, t * 4 + 1]) + (tr[g, t * 4 + 2] + tr[g, t * 4 + 3])
            others(
                a,
                lambda v, dev, mine=mine: remote(mine, mine, g_send.at[g, 3], g_recv.at[g, 3], dev).start(),
            )

    def ar4(g):
        drain(zr.at[g, pl.ds(0, 9)], g_send.at[g, 3])
        drain(zr.at[g, pl.ds(0, 9)], g_recv.at[g, 3])
        for t in range(3):
            a = (t + 1) % 3
            at = t * 16 + here[t] * 4 + here[a]
            ag[g, core, at] = ((zr[g, t * 4] + zr[g, t * 4 + 1]) + (zr[g, t * 4 + 2] + zr[g, t * 4 + 3])).astype(bf16)
            mine = ag.at[g, core, at]
            others(
                a,
                lambda v, dev, mine=mine: remote(mine, mine, g_send.at[g, 4], g_recv.at[g, 4], dev).start(),
            )

    def ar5(g):
        drain(ag.at[g, 0, pl.ds(0, 9)], g_send.at[g, 4])
        drain(ag.at[g, 0, pl.ds(0, 9)], g_recv.at[g, 4])
        for t in range(3):
            mine = ag.at[g, core, pl.ds(t * 16 + here[t] * 4, 4)]
            others(
                t,
                lambda v, dev, mine=mine: remote(mine, mine, g_send.at[g, 5], g_recv.at[g, 5], dev).start(),
            )

    def pair6(g):
        mine = ag.at[g, core]
        return remote(mine, mine, g_send.at[g, 6], g_recv.at[g, 6], partner)

    def ar6(g):
        drain(ag.at[g, 0, pl.ds(0, 36)], g_send.at[g, 5])
        drain(ag.at[g, 0, pl.ds(0, 36)], g_recv.at[g, 5])
        pair6(g).start()

    def ar7(g):
        pair6(g).wait()
        for half in range(2):
            wg_out[g, :, half * 128 : (half + 1) * 128] = ag[g, half].reshape(9 * C, 128)

    def sum_send(a):
        stat[a, me] = msg[a]

        def send(j, carry):
            remote(msg.at[a], stat.at[a, me], s_send.at[a], s_recv.at[a], peer(j)[1]).start()
            return carry

        lax.fori_loop(1, N, send, 0)

    def sum_finish(a):
        drain(stat.at[a, pl.ds(0, N - 1)], s_send.at[a])
        drain(stat.at[a, pl.ds(0, N - 1)], s_recv.at[a])
        return jnp.sum(stat[a], axis=0)

    same = (iota((C, C), 0) // (C // G) == iota((C, C), 1) // (C // G)).astype(f32)

    def per_group(v):
        wide = jnp.concatenate([v, jnp.zeros((6, C), f32)], axis=0)
        return jnp.dot(wide, same, precision=lax.Precision.HIGHEST, preferred_element_type=f32)

    parts = cb.shape[0] // HT
    slots_of = [(S_s, 0), (S_s, 1), (S_s, 2), (S_q, 0), (S_q, 1), (S_q, 2)]

    def slot_of(c):
        S, k = slots_of[c % 6]
        return S.at[k, pl.ds(0, HT)]

    def fetch(c):
        return pltpu.make_async_copy(cb.at[pl.ds(c * HT, HT)], slot_of(c), l_sems.at[c % 6])

    cot_copy = pltpu.make_async_copy(cot_hbm, S_a.at[1, pl.ds(1, HT)], l_sems.at[6])
    dec_copy = pltpu.make_async_copy(w_dec_hbm, w_dec, l_sems.at[7])
    enc_copy = pltpu.make_async_copy(w_enc_hbm, w_enc, l_sems.at[8])
    cot_copy.start()
    for c in range(6):
        fetch(c).start()
    dec_copy.start()
    enc_copy.start()

    def first(h, carry):
        v = lat[h].astype(f32)
        return carry[0] + jnp.sum(v, 0, keepdims=True), carry[1] + jnp.sum(v * v, 0, keepdims=True)

    zero = jnp.zeros((1, C), f32)
    s1, s2 = lax.fori_loop(0, HT, first, (zero, zero))
    msg[0, 0:1] = s1
    msg[0, 1:2] = s2
    cot_copy.wait()
    field_cols(S_a)

    upper = (iota((WT, WT), 0) < iota((WT, WT), 1)).astype(f32).astype(bf16)
    base = jnp.zeros((N, 1), f32)
    named = jnp.zeros((N, WT), f32)
    for h in range(HT):
        codes = ids_v[h : h + 1, :]
        member = (iota((N, WT), 0) == (codes >> 7)).astype(f32)
        member_b = member.astype(bf16)
        ahead = jnp.dot(member_b, upper, preferred_element_type=f32)
        slot = jnp.sum(member * (ahead + base), axis=0, keepdims=True)
        base = base + jnp.sum(member, axis=1, keepdims=True)
        slots[h : h + 1, :] = slot
        local = ((codes & 127) + 1).astype(f32)
        lanes = (iota((WT, WT), 0) & (CAP - 1)).astype(f32)
        spread = jnp.where(lanes == slot, local, 0.0).astype(bf16)
        named = named + lax.dot_general(member_b, spread, NT, preferred_element_type=f32)
    idrow[:, 0, :] = named - 1.0

    def ids_send(j, carry):
        t, dev = peer(j)
        remote(idrow.at[t], idr.at[me], i_send.at[0], i_recv.at[0], dev).start()
        return carry


    for c in range(parts):
        fetch(c).wait()
        S, k = slots_of[c % 6]

        def convert(h, carry, c=c, S=S, k=k):
            cbf[pl.ds(pl.multiple_of((c * HT + h) * WT, WT), WT), :] = S[k, h].astype(f32)
            return carry

        lax.fori_loop(0, HT, convert, 0)
        if c + 6 < parts:
            fetch(c + 6).start()

    pl.semaphore_wait(barrier, N - 1)
    sum_send(0)
    halo_send(COT, S_a)
    lax.fori_loop(1, N, ids_send, 0)
    idr[me] = idrow[me]

    def pick(h, carry):
        def some(t, inner):
            start = h * WT + t * 16
            for j in range(16):
                qf[t, j : j + 1, :] = cbf[pl.ds(ids_s[start + j], 1), :]
            return inner

        lax.fori_loop(0, WT // 16, some, 0)
        v = qf[...].reshape(WT, C)
        S_q[1, h + 1] = v.astype(bf16)
        qt[:, pl.ds(pl.multiple_of(h * WT, WT), WT)] = v.T.astype(bf16)
        take_cols(h, v)
        return carry

    lax.fori_loop(0, HT, pick, 0)
    halo_send(QNT, S_q)

    tot = sum_finish(0)
    grp = per_group(tot)
    mean = grp[0:1] / count
    var = grp[1:2] / count - mean * mean
    inv = lax.rsqrt(var + epsilon)
    gain_v, bias_v = gain[...], bias[...]

    def smoothing(h, carry):
        act = (lat[h].astype(f32) - mean) * inv * gain_v + bias_v
        v = act * jax.nn.sigmoid(act)
        S_s[1, h + 1] = v.astype(bf16)
        st[:, pl.ds(pl.multiple_of(h * WT, WT), WT)] = v.T.astype(bf16)
        take_cols(h, v)
        return carry

    lax.fori_loop(0, HT, smoothing, 0)
    halo_send(SMO, S_s)

    halo_finish(COT, S_a)
    dec_copy.wait()
    enc_copy.wait()
    wgrad(0, qt, S_a)
    convt(S_a, w_dec, lambda r0, v: put(BQ, r0, v))
    halo_finish(SMO, S_s)

    def keep_enc(r0, v):
        put(ENC, r0, v + lat[pl.ds(r0, RB)].reshape(RB * WT, C).astype(f32))

    conv(S_s, w_enc, keep_enc)
    ar1(0)

    def keep_dec(r0, v):
        dec_out[pl.ds(r0, RB)] = v.reshape(RB, WT, C).astype(bf16)

    code_scale = float(16384) / (HT * WT * N)

    def rotate(h, carry):
        for k in range(4):
            at = slice(k * 32, (k + 1) * 32)
            there = pl.ds(pl.multiple_of(h * WT + k * 32, 32), 32)
            z, b = cbf[pl.ds(pl.multiple_of(ENC + h * WT + k * 32, 32), 32), :], cbf[there, :]
            e = S_q[1, h + 1, at].astype(f32)
            z_norm = jnp.sqrt(jnp.sum(z * z, -1, keepdims=True) + epsilon)
            e_norm = jnp.sqrt(jnp.sum(e * e, -1, keepdims=True) + epsilon)
            z_unit = z * (1.0 / z_norm)
            e_unit = e * (1.0 / e_norm)
            mirror = z_unit + e_unit
            mirror = mirror * (1.0 / jnp.sqrt(jnp.sum(mirror * mirror, -1, keepdims=True) + epsilon))
            along_mirror = jnp.sum(mirror * b, -1, keepdims=True)
            along_code = jnp.sum(e_unit * b, -1, keepdims=True)
            turned = b - (2.0 * along_mirror) * mirror + (2.0 * along_code) * z_unit
            back = (e_norm / z_norm) * turned + commit_beta * (z - e)
            cbf[pl.ds(pl.multiple_of(EB + h * WT + k * 32, 32), 32), :] = back
            S_a[1, h + 1, at] = back.astype(bf16)
            pull[there, :] = (code_scale * (e - z)).astype(bf16)
            if k == 0:
                colf[0, pl.ds(h, 1)] = back[0:1]
            if k == 3:
                colf[1, pl.ds(h, 1)] = back[31:32]
        return carry

    lax.fori_loop(0, HT, rotate, 0)
    halo_send(BCK, S_a)
    ar2(0)
    halo_finish(QNT, S_q)

    for h in range(HT):
        at = slice(h * WT, (h + 1) * WT)
        dkey[:, at] = jnp.broadcast_to((ids_v[h : h + 1, :] >> 7).astype(f32), (16, WT)).astype(bf16)
        skey[:, at] = jnp.broadcast_to(slots[h : h + 1, :], (16, WT)).astype(bf16)
    low = iota((16, POS), 0).astype(f32).astype(bf16)
    one, nil, gone = jnp.ones((16, POS), bf16), jnp.zeros((16, POS), bf16), jnp.full((16, POS), -1.0, bf16)

    def pack(i, carry):
        first_owner = lax.rem(me // 8 + i, N // 8) * 8
        parts = []
        for j in range(8):
            owner = jnp.full((16, POS), (first_owner + j).astype(f32), f32).astype(bf16)
            key = jnp.where(dkey[...] == owner, skey[...], gone)
            parts.append(jnp.where(key == low, one, nil))
            parts.append(jnp.where(key == low + 16.0, one, nil))
        select = jnp.concatenate(parts, axis=0)
        rows = jnp.dot(select, pull[...], preferred_element_type=f32)
        sb[pl.ds(first_owner, 8)] = rows.reshape(8, CAP, C).astype(bf16)
        return carry

    def send_block(i):
        first_owner = lax.rem(me // 8 + i, N // 8) * 8

        def go(j, carry):
            t = first_owner + j

            @pl.when(t != me)
            def _():
                dev = {"row": t // NC, "col": lax.rem(t, NC)}
                remote(sb.at[t], rb.at[me], c_send.at[0], c_recv.at[0], dev).start()

            return carry

        lax.fori_loop(0, 8, go, 0)

    def send_blocks(a, b):
        def go(i, carry):
            send_block(i)
            return carry

        lax.fori_loop(a, b, go, 0)

    def pack_send(i, carry):
        pack(i, carry)
        send_block(i)
        return carry

    lax.fori_loop(0, 6, pack_send, 0)

    ar3(0)

    halo_finish(BCK, S_a)
    wgrad(1, st, S_a)
    ar1(1)
    lax.fori_loop(6, 9, pack_send, 0)
    lax.fori_loop(9, N // 8, pack, 0)
    rb[me] = sb[me]
    ar4(0)
    ar2(1)
    send_blocks(9, 11)

    def backward(r0, v):
        bs = v.reshape(RB, WT, C)
        s_b, s_g = zero, zero
        for k in range(RB):
            normed = (lat[r0 + k].astype(f32) - mean) * inv
            act = normed * gain_v + bias_v
            s = jax.nn.sigmoid(act)
            t = bs[k] * s * (1.0 + act * (1.0 - s))
            put(BA, r0 + k, t)
            s_b = s_b + jnp.sum(t, 0, keepdims=True)
            s_g = s_g + jnp.sum(t * normed, 0, keepdims=True)
        msg[1, 0:1] += s_b
        msg[1, 1:2] += s_g

    msg[1] = jnp.zeros((2, C), f32)
    convt(S_a, w_enc, backward)
    sum_send(1)
    ar3(1)
    send_blocks(11, 13)
    ar5(0)
    conv(S_q, w_dec, keep_dec)
    ar4(1)
    send_blocks(13, 16)
    ar6(0)

    tot2 = sum_finish(1)
    gsum_out[...] = tot2
    means = per_group(tot2 * gain_v) * (1.0 / count)
    mean1, mean2 = means[0:1], means[1:2]

    def last(h, carry):
        normed = (lat[h].astype(f32) - mean) * inv
        lg_out[h] = (inv * (row_of(BA, h) * gain_v - mean1 - normed * mean2) + row_of(EB, h)).astype(bf16)
        return carry

    lax.fori_loop(0, HT, last, 0)
    ar5(1)
    ar7(0)
    ar6(1)

    drain(idr.at[pl.ds(0, N - 1)], i_send.at[0])
    drain(idr.at[pl.ds(0, N - 1)], i_recv.at[0])
    drain(sb.at[pl.ds(0, N - 1)], c_send.at[0])
    drain(rb.at[pl.ds(0, N - 1)], c_recv.at[0])
    quarter = iota((1, WT), 1) // CAP

    def collect(g, acc):
        hot = []
        for half in range(2):
            names = idr[g * 8 + half * 4]
            for j in range(1, 4):
                names = jnp.where(quarter == j, idr[g * 8 + half * 4 + j], names)
            hot.append((iota((N, WT), 0).astype(f32) == names).astype(f32).astype(bf16))
        rows = rb[pl.ds(g * 8, 8)].reshape(8 * CAP, C)
        return acc + jnp.dot(jnp.concatenate(hot, axis=1), rows, preferred_element_type=f32)

    cg_out[...] = lax.fori_loop(0, N // 8, collect, jnp.zeros((N, C), f32))
    ar7(1)


def main(lat, code_ids, gain, bias, w_enc, w_dec, cot, codebook):
    dma = pltpu.SemaphoreType.DMA
    V = pltpu.VMEM
    field = V((3, HT + 2, WT, C), bf16)
    return pl.pallas_call(
        main_kernel,
        out_shape=(
            jax.ShapeDtypeStruct((HT, WT, C), bf16),
            jax.ShapeDtypeStruct((HT, WT, C), bf16),
            jax.ShapeDtypeStruct((2, C), f32),
            jax.ShapeDtypeStruct((2, 9 * C, C), bf16),
            jax.ShapeDtypeStruct((N, C), f32),
        ),
        in_specs=[VM, SM, VM, VM, VM, ANY, ANY, ANY, ANY],
        out_specs=(VM,) * 5,
        scratch_shapes=[
            field, field, field,
            V((4, 2, WT, C), bf16), V((4, 6, HT, C), bf16), V((4, 2, HT, C), bf16),
            V((2, HT, C), f32), V((2, 32, C), f32),
            V((codebook.shape[0] * WT, C), f32), V((WT // 16, 16, C), f32), V((HT, WT), f32),
            V((N, 1, WT), f32), V((C, POS), bf16), V((9, C, C), bf16), V((9, C, C), bf16),
            V((POS, C), bf16), V((C, POS), bf16),
            V((2, 2, C), f32), V((2, N, 2, C), f32),
            V((N, CAP, C), bf16), V((N, CAP, C), bf16), V((N, 1, WT), f32),
            V((16, POS), bf16), V((16, POS), bf16),
            V((2, 2, 9 * C, 128), f32), V((2, 9 * C, 128), f32),
            V((2, 12, 192, 128), f32), V((2, 12, 192, 128), f32), V((2, 12, 48, 128), f32), V((2, 12, 48, 128), f32),
            V((2, 12, 48, 128), f32), V((2, 2, 48, 48, 128), bf16),
            dma((9,)), dma((4, 8)), dma((4, 8)), dma((2,)), dma((2,)), dma((1,)), dma((1,)), dma((1,)), dma((1,)),
            dma((2, 3)), dma((2, 3)), dma((2, 7)), dma((2, 7)),
        ],
        compiler_params=pltpu.CompilerParams(
            collective_id=0, has_side_effects=True, vmem_limit_bytes=67_000_000
        ),
        name="main",
    )(lat, code_ids.reshape(POS), code_ids, gain, bias, w_enc, w_dec, cot, codebook)


def body(latents, code_ids, norm_gain, norm_bias, encoder_weight, codebook, decoder_weight, cotangent):
    decoded, latents_grad, gsum, wg, cg = main(
        latents, code_ids, norm_gain.reshape(1, C), norm_bias.reshape(1, C),
        encoder_weight.reshape(9, C, C), decoder_weight.reshape(9, C, C), cotangent, codebook.reshape(-1, WT, C),
    )
    wg = wg.reshape(2, 3, 3, C, C).astype(f32)
    return decoded, latents_grad, gsum[1], gsum[0], wg[1], wg[0], cg


def solution(mesh):
    tiled = P("row", "col", None)
    in_specs = (tiled, P("row", "col"), P(), P(), P(), P(), P(), tiled)
    out_specs = (tiled, tiled, P(), P(), P(), P(), P(("row", "col"), None))
    return jax.shard_map(body, mesh=mesh, in_specs=in_specs, out_specs=out_specs, check_vma=False)
```

```python
import functools

import jax
import jax.numpy as jnp
from jax import lax
from jax.experimental import pallas as pl
from jax.experimental.pallas import tpu as pltpu
from jax.sharding import PartitionSpec as P

G = 32
NR, NC = 16, 8
N = NR * NC
HT, WT, C = 16, 128, 256
POS = HT * WT
CAP = 32
epsilon = 1e-06
commit_beta = 0.25
f32, bf16, i32 = jnp.float32, jnp.bfloat16, jnp.int32
MESH = pl.DeviceIdType.MESH
VM = pl.BlockSpec(memory_space=pltpu.VMEM)
SM = pl.BlockSpec(memory_space=pltpu.SMEM)
ANY = pl.BlockSpec(memory_space=pl.ANY)
NT = (((1,), (1,)), ((), ()))


def iota(shape, dim):
    return lax.broadcasted_iota(i32, shape, dim)


COT, QNT, SMO, BCK = 0, 1, 2, 3


def main_kernel(
    lat, ids_s, ids_v, gain, bias, w_enc_hbm, w_dec_hbm, cot_hbm, cb,
    dec_hbm, lg_hbm, gsum_out, wg_out, cg_out,
    dec_out, lg_out,
    S_a, S_q, S_s, hr, hc, hs, colf, cf,
    cbf, qf, slots, idrow, qt, w_enc, w_dec, pull, st,
    msg, stat, sb, rb, idr, dkey, skey,
    grad, p0r, rss, rsr, tb, tr, zr, ag,
    l_sems, h_send, h_recv, s_send, s_recv, i_send, i_recv, c_send, c_recv, p_send, p_recv, g_send, g_recv,
):
    row, col = lax.axis_index("row"), lax.axis_index("col")
    me = row * NC + col
    core = lax.rem(row, 2)
    zed = lax.rem(row // 2, 4)
    ylo = row // 8
    up, dn = lax.rem(row + NR - 1, NR), lax.rem(row + 1, NR)
    lf, rt = lax.rem(col + NC - 1, NC), lax.rem(col + 1, NC)
    count = float(HT * WT * N * (C // G))

    barrier = pltpu.get_barrier_semaphore()

    cols = [col] + [lax.rem(col + c, NC) for c in range(1, NC)]

    def each_peer(act):
        for c in range(1, NC):
            act(row, cols[c])

        def go(r, carry):
            other = lax.rem(row + r, NR)
            for c in range(NC):
                act(other, cols[c])
            return carry

        lax.fori_loop(1, NR, go, 0)

    each_peer(
        lambda r, c: pl.semaphore_signal(barrier, inc=1, device_id={"row": r, "col": c}, device_id_type=MESH)
    )

    def remote(src, dst, ss, rs, dev):
        return pltpu.make_async_remote_copy(
            src_ref=src, dst_ref=dst, send_sem=ss, recv_sem=rs, device_id=dev, device_id_type=MESH
        )

    def drain(ref, sem):
        pltpu.make_async_copy(ref, ref, sem).wait()

    def halo_copies(f, S):
        here = {
            0: (S.at[1, HT], hr.at[f, 0], dn, col),
            1: (S.at[1, 1], hr.at[f, 1], up, col),
            2: (hs.at[f, 1], hc.at[f, 1], row, rt),
            3: (hs.at[f, 1], hc.at[f, 0], dn, rt),
            4: (hs.at[f, 1], hc.at[f, 2], up, rt),
            5: (hs.at[f, 0], hc.at[f, 4], row, lf),
            6: (hs.at[f, 0], hc.at[f, 3], dn, lf),
            7: (hs.at[f, 0], hc.at[f, 5], up, lf),
        }
        return [
            remote(s, d, h_send.at[f, k], h_recv.at[f, k], {"row": r, "col": c})
            for k, (s, d, r, c) in here.items()
        ]

    def halo_send(f, S):
        hs[f] = colf[...].astype(bf16)
        for copy in halo_copies(f, S):
            copy.start()

    ok_u = jnp.where(row > 0, 1.0, 0.0).astype(f32)
    ok_d = jnp.where(row < NR - 1, 1.0, 0.0).astype(f32)
    ok_l = jnp.where(col > 0, 1.0, 0.0).astype(f32)
    ok_r = jnp.where(col < NC - 1, 1.0, 0.0).astype(f32)

    def halo_finish(f, S):
        for copy in halo_copies(f, S):
            copy.wait()
        S[1, 0] = (hr[f, 0].astype(f32) * ok_u).astype(bf16)
        S[1, HT + 1] = (hr[f, 1].astype(f32) * ok_d).astype(bf16)
        for side, ok in ((0, ok_l), (1, ok_r)):
            above = hc[f, 3 * side].astype(f32) * (ok * ok_u)
            below = hc[f, 3 * side + 2].astype(f32) * (ok * ok_d)
            cf[side, 8:24] = hc[f, 3 * side + 1].astype(f32) * ok
            cf[side, 7:8] = above[15:16]
            cf[side, 24:25] = below[0:1]

        def shift(hh, carry):
            v = S[1, hh].astype(f32)
            place = iota((WT, C), 0)
            S[0, hh] = jnp.where(place == 0, cf[0, pl.ds(hh + 7, 1)], pltpu.roll(v, 1, 0)).astype(bf16)
            S[2, hh] = jnp.where(
                place == WT - 1, cf[1, pl.ds(hh + 7, 1)], pltpu.roll(v, WT - 1, 0)
            ).astype(bf16)
            return carry

        lax.fori_loop(0, HT + 2, shift, 0)

    def take_cols(h, v):
        colf[0, pl.ds(h, 1)] = v[0:1]
        colf[1, pl.ds(h, 1)] = v[WT - 1 : WT]

    def field_cols(S):
        def body(h, carry):
            take_cols(h, S[1, h + 1].astype(f32))
            return carry

        lax.fori_loop(0, HT, body, 0)

    BQ, ENC, EB, BA = 0, POS, 2 * POS, 3 * POS

    def put(plane, r0, v):
        cbf[pl.ds(pl.multiple_of(plane + r0 * WT, WT), v.shape[0]), :] = v

    def row_of(plane, h):
        return cbf[pl.ds(pl.multiple_of(plane + h * WT, WT), WT), :]

    RB = 4

    def windows(S, r0, flip):
        parts = []
        for dy in range(3):
            for dx in range(3):
                a, b = (2 - dx, 2 - dy) if flip else (dx, dy)
                parts.append(S[a, pl.ds(r0 + b, RB)].reshape(RB * WT, C))
        return jnp.concatenate(parts, axis=1)

    def conv(S, w, use):
        def body(i, carry):
            r0 = i * RB
            use(r0, jnp.dot(windows(S, r0, False), w[...].reshape(9 * C, C), preferred_element_type=f32))
            return carry

        lax.fori_loop(0, HT // RB, body, 0)

    def convt(S, w, use):
        def body(i, carry):
            r0 = i * RB
            wide = jnp.concatenate([w[k] for k in range(9)], axis=1)
            use(r0, lax.dot_general(windows(S, r0, True), wide, NT, preferred_element_type=f32))
            return carry

        lax.fori_loop(0, HT // RB, body, 0)

    partner = {"row": row + 1 - 2 * core, "col": col}

    here = (lax.rem(col, 4), (col // 4) * 2 + ylo, zed)

    def along(axis, v):
        if axis == 0:
            return {"row": row, "col": (col // 4) * 4 + v}
        if axis == 1:
            return {"row": lax.rem(v, 2) * 8 + lax.rem(row, 8), "col": (v // 2) * 4 + lax.rem(col, 4)}
        return {"row": ylo * 8 + v * 2 + core, "col": col}

    def others(axis, send):
        def go(j, carry):
            t = lax.rem(here[axis] + j, 4)
            send(t, along(axis, t))
            return carry

        lax.fori_loop(1, 4, go, 0)

    def pair0(g, t):
        at = pl.ds(t * 768, 768)
        return remote(grad.at[g, 1 - core, at], p0r.at[g, at], p_send.at[g, t], p_recv.at[g, t], partner)

    def wgrad(g, ut, S):
        for dy in range(3):

            def body(dx, carry, dy=dy):
                win = S[2 - dx, 2 - dy : 2 - dy + HT].reshape(POS, C)
                res = jnp.dot(ut[...], win, preferred_element_type=f32)
                at = pl.ds(pl.multiple_of((dy * 3 + dx) * C, C), C)
                grad[g, 0, at, :] = res[:, :128]
                grad[g, 1, at, :] = res[:, 128:]
                return carry

            lax.fori_loop(0, 3, body, 0)
            pair0(g, dy).start()

    def ar1(g):
        for t in range(3):
            pair0(g, t).wait()

            def add(j, carry, t=t):
                at = pl.ds(pl.multiple_of((t * 4 + j) * 192, 64), 192)
                rss[g, t * 4 + j] = grad[g, core, at, :] + p0r[g, at, :]
                return carry

            lax.fori_loop(0, 4, add, 0)
            mine = t * 4 + here[t]
            rsr[g, mine] = rss[g, mine]
            others(
                t,
                lambda v, dev, t=t, mine=mine: remote(
                    rss.at[g, t * 4 + v], rsr.at[g, mine], g_send.at[g, 1], g_recv.at[g, 1], dev
                ).start(),
            )

    def ar2(g):
        drain(rss.at[g, pl.ds(0, 9)], g_send.at[g, 1])
        drain(rsr.at[g, pl.ds(0, 9)], g_recv.at[g, 1])
        for t in range(3):
            for c in range(4):
                at = slice(c * 48, (c + 1) * 48)
                tb[g, t * 4 + c] = (rsr[g, t * 4, at] + rsr[g, t * 4 + 1, at]) + (
                    rsr[g, t * 4 + 2, at] + rsr[g, t * 4 + 3, at]
                )
        for t in range(3):
            a = (t + 1) % 3
            mine = t * 4 + here[a]
            tr[g, mine] = tb[g, mine]
            others(
                a,
                lambda v, dev, t=t, mine=mine: remote(
                    tb.at[g, t * 4 + v], tr.at[g, mine], g_send.at[g, 2], g_recv.at[g, 2], dev
                ).start(),
            )

    def ar3(g):
        drain(tb.at[g, pl.ds(0, 9)], g_send.at[g, 2])
        drain(tr.at[g, pl.ds(0, 9)], g_recv.at[g, 2])
        for t in range(3):
            a = (t + 2) % 3
            mine = zr.at[g, t * 4 + here[a]]
            zr[g, t * 4 + here[a]] = (tr[g, t * 4] + tr[g, t * 4 + 1]) + (tr[g, t * 4 + 2] + tr[g, t * 4 + 3])
            others(
                a,
                lambda v, dev, mine=mine: remote(mine, mine, g_send.at[g, 3], g_recv.at[g, 3], dev).start(),
            )

    def ar4(g):
        drain(zr.at[g, pl.ds(0, 9)], g_send.at[g, 3])
        drain(zr.at[g, pl.ds(0, 9)], g_recv.at[g, 3])
        for t in range(3):
            a = (t + 1) % 3
            at = t * 16 + here[t] * 4 + here[a]
            ag[g, core, at] = ((zr[g, t * 4] + zr[g, t * 4 + 1]) + (zr[g, t * 4 + 2] + zr[g, t * 4 + 3])).astype(bf16)
            mine = ag.at[g, core, at]
            others(
                a,
                lambda v, dev, mine=mine: remote(mine, mine, g_send.at[g, 4], g_recv.at[g, 4], dev).start(),
            )

    def ar5(g):
        drain(ag.at[g, 0, pl.ds(0, 9)], g_send.at[g, 4])
        drain(ag.at[g, 0, pl.ds(0, 9)], g_recv.at[g, 4])
        for t in range(3):
            mine = ag.at[g, core, pl.ds(t * 16 + here[t] * 4, 4)]
            others(
                t,
                lambda v, dev, mine=mine: remote(mine, mine, g_send.at[g, 5], g_recv.at[g, 5], dev).start(),
            )

    def pair6(g):
        mine = ag.at[g, core]
        return remote(mine, mine, g_send.at[g, 6], g_recv.at[g, 6], partner)

    def ar6(g):
        drain(ag.at[g, 0, pl.ds(0, 36)], g_send.at[g, 5])
        drain(ag.at[g, 0, pl.ds(0, 36)], g_recv.at[g, 5])
        pair6(g).start()

    def ar7(g):
        pair6(g).wait()
        for half in range(2):
            wg_out[g, :, half * 128 : (half + 1) * 128] = ag[g, half].reshape(9 * C, 128)

    def sum_send(a):
        stat[a, me] = msg[a]

        each_peer(
            lambda r, c: remote(
                msg.at[a], stat.at[a, me], s_send.at[a], s_recv.at[a], {"row": r, "col": c}
            ).start()
        )

    def sum_finish(a):
        drain(stat.at[a, pl.ds(0, N - 1)], s_send.at[a])
        drain(stat.at[a, pl.ds(0, N - 1)], s_recv.at[a])
        return jnp.sum(stat[a], axis=0)

    same = (iota((C, C), 0) // (C // G) == iota((C, C), 1) // (C // G)).astype(f32)

    def per_group(v):
        wide = jnp.concatenate([v, jnp.zeros((6, C), f32)], axis=0)
        return jnp.dot(wide, same, precision=lax.Precision.HIGHEST, preferred_element_type=f32)

    parts = cb.shape[0] // HT
    slots_of = [(S_s, 0), (S_s, 1), (S_s, 2), (S_q, 0), (S_q, 1), (S_q, 2)]

    def slot_of(c):
        S, k = slots_of[c % 6]
        return S.at[k, pl.ds(0, HT)]

    def fetch(c):
        return pltpu.make_async_copy(cb.at[pl.ds(c * HT, HT)], slot_of(c), l_sems.at[c % 6])

    cot_copy = pltpu.make_async_copy(cot_hbm, S_a.at[1, pl.ds(1, HT)], l_sems.at[6])
    dec_copy = pltpu.make_async_copy(w_dec_hbm, w_dec, l_sems.at[7])
    enc_copy = pltpu.make_async_copy(w_enc_hbm, w_enc, l_sems.at[8])
    cot_copy.start()
    for c in range(6):
        fetch(c).start()
    dec_copy.start()
    enc_copy.start()

    def first(h, carry):
        v = lat[h].astype(f32)
        return carry[0] + jnp.sum(v, 0, keepdims=True), carry[1] + jnp.sum(v * v, 0, keepdims=True)

    zero = jnp.zeros((1, C), f32)
    s1, s2 = lax.fori_loop(0, HT, first, (zero, zero))
    msg[0, 0:1] = s1
    msg[0, 1:2] = s2
    cot_copy.wait()
    field_cols(S_a)

    upper = (iota((WT, WT), 0) < iota((WT, WT), 1)).astype(f32).astype(bf16)
    base = jnp.zeros((N, 1), f32)
    named = jnp.zeros((N, WT), f32)
    for h in range(HT):
        codes = ids_v[h : h + 1, :]
        member = (iota((N, WT), 0) == (codes >> 7)).astype(f32)
        member_b = member.astype(bf16)
        ahead = jnp.dot(member_b, upper, preferred_element_type=f32)
        slot = jnp.sum(member * (ahead + base), axis=0, keepdims=True)
        base = base + jnp.sum(member, axis=1, keepdims=True)
        slots[h : h + 1, :] = slot
        local = ((codes & 127) + 1).astype(f32)
        lanes = (iota((WT, WT), 0) & (CAP - 1)).astype(f32)
        spread = jnp.where(lanes == slot, local, 0.0).astype(bf16)
        named = named + lax.dot_general(member_b, spread, NT, preferred_element_type=f32)
    idrow[:, 0, :] = named - 1.0

    for c in range(parts):
        fetch(c).wait()
        S, k = slots_of[c % 6]

        def convert(h, carry, c=c, S=S, k=k):
            cbf[pl.ds(pl.multiple_of((c * HT + h) * WT, WT), WT), :] = S[k, h].astype(f32)
            return carry

        lax.fori_loop(0, HT, convert, 0)
        if c + 6 < parts:
            fetch(c + 6).start()

    pl.semaphore_wait(barrier, N - 1)
    sum_send(0)
    halo_send(COT, S_a)
    each_peer(
        lambda r, c: remote(
            idrow.at[r * NC + c], idr.at[me], i_send.at[0], i_recv.at[0], {"row": r, "col": c}
        ).start()
    )
    idr[me] = idrow[me]

    def pick(h, carry):
        def some(t, inner):
            start = h * WT + t * 16
            for j in range(16):
                qf[t, j : j + 1, :] = cbf[pl.ds(ids_s[start + j], 1), :]
            return inner

        lax.fori_loop(0, WT // 16, some, 0)
        v = qf[...].reshape(WT, C)
        S_q[1, h + 1] = v.astype(bf16)
        qt[:, pl.ds(pl.multiple_of(h * WT, WT), WT)] = v.T.astype(bf16)
        take_cols(h, v)
        return carry

    lax.fori_loop(0, HT, pick, 0)
    halo_send(QNT, S_q)

    tot = sum_finish(0)
    grp = per_group(tot)
    mean = grp[0:1] / count
    var = grp[1:2] / count - mean * mean
    inv = lax.rsqrt(var + epsilon)
    gain_v, bias_v = gain[...], bias[...]

    def smoothing(h, carry):
        act = (lat[h].astype(f32) - mean) * inv * gain_v + bias_v
        v = act * jax.nn.sigmoid(act)
        S_s[1, h + 1] = v.astype(bf16)
        st[:, pl.ds(pl.multiple_of(h * WT, WT), WT)] = v.T.astype(bf16)
        take_cols(h, v)
        return carry

    lax.fori_loop(0, HT, smoothing, 0)
    halo_send(SMO, S_s)

    halo_finish(COT, S_a)
    dec_copy.wait()
    enc_copy.wait()
    wgrad(0, qt, S_a)
    convt(S_a, w_dec, lambda r0, v: put(BQ, r0, v))
    halo_finish(SMO, S_s)

    def keep_enc(r0, v):
        put(ENC, r0, v + lat[pl.ds(r0, RB)].reshape(RB * WT, C).astype(f32))

    conv(S_s, w_enc, keep_enc)
    ar1(0)

    def keep_dec(r0, v):
        dec_out[pl.ds(r0, RB)] = v.reshape(RB, WT, C).astype(bf16)

    code_scale = float(16384) / (HT * WT * N)

    def rotate(h, carry):
        for k in range(4):
            at = slice(k * 32, (k + 1) * 32)
            there = pl.ds(pl.multiple_of(h * WT + k * 32, 32), 32)
            z, b = cbf[pl.ds(pl.multiple_of(ENC + h * WT + k * 32, 32), 32), :], cbf[there, :]
            e = S_q[1, h + 1, at].astype(f32)
            z_square = jnp.sum(z * z, -1, keepdims=True) + epsilon
            e_square = jnp.sum(e * e, -1, keepdims=True) + epsilon
            z_over, e_over = lax.rsqrt(z_square), lax.rsqrt(e_square)
            z_unit = z * z_over
            e_unit = e * e_over
            mirror = z_unit + e_unit
            mirror = mirror * lax.rsqrt(jnp.sum(mirror * mirror, -1, keepdims=True) + epsilon)
            along_mirror = jnp.sum(mirror * b, -1, keepdims=True)
            along_code = jnp.sum(e_unit * b, -1, keepdims=True)
            turned = b - (2.0 * along_mirror) * mirror + (2.0 * along_code) * z_unit
            back = (e_square * e_over * z_over) * turned + commit_beta * (z - e)
            cbf[pl.ds(pl.multiple_of(EB + h * WT + k * 32, 32), 32), :] = back
            S_a[1, h + 1, at] = back.astype(bf16)
            pull[there, :] = (code_scale * (e - z)).astype(bf16)
            if k == 0:
                colf[0, pl.ds(h, 1)] = back[0:1]
            if k == 3:
                colf[1, pl.ds(h, 1)] = back[31:32]
        return carry

    lax.fori_loop(0, HT, rotate, 0)
    halo_send(BCK, S_a)
    ar2(0)
    halo_finish(QNT, S_q)

    for h in range(HT):
        at = slice(h * WT, (h + 1) * WT)
        dkey[:, at] = jnp.broadcast_to((ids_v[h : h + 1, :] >> 7).astype(f32), (16, WT)).astype(bf16)
        skey[:, at] = jnp.broadcast_to(slots[h : h + 1, :], (16, WT)).astype(bf16)
    low = iota((16, POS), 0).astype(f32).astype(bf16)
    one, nil, gone = jnp.ones((16, POS), bf16), jnp.zeros((16, POS), bf16), jnp.full((16, POS), -1.0, bf16)

    def pack(i, carry):
        first_owner = lax.rem(row + i, NR) * NC
        parts = []
        for j in range(8):
            owner = jnp.full((16, POS), (first_owner + j).astype(f32), f32).astype(bf16)
            key = jnp.where(dkey[...] == owner, skey[...], gone)
            parts.append(jnp.where(key == low, one, nil))
            parts.append(jnp.where(key == low + 16.0, one, nil))
        select = jnp.concatenate(parts, axis=0)
        rows = jnp.dot(select, pull[...], preferred_element_type=f32)
        sb[pl.ds(first_owner, 8)] = rows.reshape(8, CAP, C).astype(bf16)
        return carry

    def send_block(i):
        other = lax.rem(row + i, NR)

        def one_row(c):
            remote(
                sb.at[other * NC + cols[c]], rb.at[me], c_send.at[0], c_recv.at[0], {"row": other, "col": cols[c]}
            ).start()

        @pl.when(i > 0)
        def _():
            one_row(0)

        for c in range(1, NC):
            one_row(c)

    def send_blocks(a, b):
        def go(i, carry):
            send_block(i)
            return carry

        lax.fori_loop(a, b, go, 0)

    def pack_send(i, carry):
        pack(i, carry)
        send_block(i)
        return carry

    lax.fori_loop(0, 6, pack_send, 0)

    ar3(0)

    halo_finish(BCK, S_a)
    wgrad(1, st, S_a)
    ar1(1)
    lax.fori_loop(6, 9, pack_send, 0)
    lax.fori_loop(9, N // 8, pack, 0)
    rb[me] = sb[me]
    ar4(0)
    ar2(1)
    send_blocks(9, 11)

    def backward(r0, v):
        bs = v.reshape(RB, WT, C)
        s_b, s_g = zero, zero
        for k in range(RB):
            normed = (lat[r0 + k].astype(f32) - mean) * inv
            act = normed * gain_v + bias_v
            s = jax.nn.sigmoid(act)
            t = bs[k] * s * (1.0 + act * (1.0 - s))
            put(BA, r0 + k, t)
            s_b = s_b + jnp.sum(t, 0, keepdims=True)
            s_g = s_g + jnp.sum(t * normed, 0, keepdims=True)
        msg[1, 0:1] += s_b
        msg[1, 1:2] += s_g

    msg[1] = jnp.zeros((2, C), f32)
    convt(S_a, w_enc, backward)
    sum_send(1)
    ar3(1)
    send_blocks(11, 13)
    ar5(0)
    conv(S_q, w_dec, keep_dec)
    dec_back = pltpu.make_async_copy(dec_out, dec_hbm, l_sems.at[9])
    dec_back.start()
    ar4(1)
    send_blocks(13, 15)
    ar6(0)

    tot2 = sum_finish(1)
    gsum_out[...] = tot2
    means = per_group(tot2 * gain_v) * (1.0 / count)
    mean1, mean2 = means[0:1], means[1:2]

    def last(h, carry):
        normed = (lat[h].astype(f32) - mean) * inv
        lg_out[h] = (inv * (row_of(BA, h) * gain_v - mean1 - normed * mean2) + row_of(EB, h)).astype(bf16)
        return carry

    lax.fori_loop(0, HT, last, 0)
    lg_back = pltpu.make_async_copy(lg_out, lg_hbm, l_sems.at[10])
    lg_back.start()
    ar5(1)
    send_blocks(15, 16)
    ar7(0)
    ar6(1)

    drain(idr.at[pl.ds(0, N - 1)], i_send.at[0])
    drain(idr.at[pl.ds(0, N - 1)], i_recv.at[0])
    drain(sb.at[pl.ds(0, N - 1)], c_send.at[0])
    drain(rb.at[pl.ds(0, N - 1)], c_recv.at[0])
    quarter = iota((1, WT), 1) // CAP

    def collect(g, acc):
        hot = []
        for half in range(2):
            names = idr[g * 8 + half * 4]
            for j in range(1, 4):
                names = jnp.where(quarter == j, idr[g * 8 + half * 4 + j], names)
            hot.append((iota((N, WT), 0).astype(f32) == names).astype(f32).astype(bf16))
        rows = rb[pl.ds(g * 8, 8)].reshape(8 * CAP, C)
        return acc + jnp.dot(jnp.concatenate(hot, axis=1), rows, preferred_element_type=f32)

    cg_out[...] = lax.fori_loop(0, N // 8, collect, jnp.zeros((N, C), f32))
    ar7(1)
    dec_back.wait()
    lg_back.wait()


def main(lat, code_ids, gain, bias, w_enc, w_dec, cot, codebook):
    dma = pltpu.SemaphoreType.DMA
    V = pltpu.VMEM
    field = V((3, HT + 2, WT, C), bf16)
    return pl.pallas_call(
        main_kernel,
        out_shape=(
            jax.ShapeDtypeStruct((HT, WT, C), bf16),
            jax.ShapeDtypeStruct((HT, WT, C), bf16),
            jax.ShapeDtypeStruct((2, C), f32),
            jax.ShapeDtypeStruct((2, 9 * C, C), bf16),
            jax.ShapeDtypeStruct((N, C), f32),
        ),
        in_specs=[VM, SM, VM, VM, VM, ANY, ANY, ANY, ANY],
        out_specs=(ANY, ANY, VM, VM, VM),
        scratch_shapes=[
            V((HT, WT, C), bf16), V((HT, WT, C), bf16),
            field, field, field,
            V((4, 2, WT, C), bf16), V((4, 6, HT, C), bf16), V((4, 2, HT, C), bf16),
            V((2, HT, C), f32), V((2, 32, C), f32),
            V((codebook.shape[0] * WT, C), f32), V((WT // 16, 16, C), f32), V((HT, WT), f32),
            V((N, 1, WT), f32), V((C, POS), bf16), V((9, C, C), bf16), V((9, C, C), bf16),
            V((POS, C), bf16), V((C, POS), bf16),
            V((2, 2, C), f32), V((2, N, 2, C), f32),
            V((N, CAP, C), bf16), V((N, CAP, C), bf16), V((N, 1, WT), f32),
            V((16, POS), bf16), V((16, POS), bf16),
            V((2, 2, 9 * C, 128), f32), V((2, 9 * C, 128), f32),
            V((2, 12, 192, 128), f32), V((2, 12, 192, 128), f32), V((2, 12, 48, 128), f32), V((2, 12, 48, 128), f32),
            V((2, 12, 48, 128), f32), V((2, 2, 48, 48, 128), bf16),
            dma((11,)), dma((4, 8)), dma((4, 8)), dma((2,)), dma((2,)), dma((1,)), dma((1,)), dma((1,)), dma((1,)),
            dma((2, 3)), dma((2, 3)), dma((2, 7)), dma((2, 7)),
        ],
        compiler_params=pltpu.CompilerParams(
            collective_id=0, has_side_effects=True, vmem_limit_bytes=67_000_000
        ),
        name="main",
    )(lat, code_ids.reshape(POS), code_ids, gain, bias, w_enc, w_dec, cot, codebook)


def body(latents, code_ids, norm_gain, norm_bias, encoder_weight, codebook, decoder_weight, cotangent):
    decoded, latents_grad, gsum, wg, cg = main(
        latents, code_ids, norm_gain.reshape(1, C), norm_bias.reshape(1, C),
        encoder_weight.reshape(9, C, C), decoder_weight.reshape(9, C, C), cotangent, codebook.reshape(-1, WT, C),
    )
    wg = wg.reshape(2, 3, 3, C, C).astype(f32)
    return decoded, latents_grad, gsum[1], gsum[0], wg[1], wg[0], cg


def solution(mesh):
    tiled = P("row", "col", None)
    in_specs = (tiled, P("row", "col"), P(), P(), P(), P(), P(), tiled)
    out_specs = (tiled, tiled, P(), P(), P(), P(), P(("row", "col"), None))
    return jax.shard_map(body, mesh=mesh, in_specs=in_specs, out_specs=out_specs, check_vma=False)
```

```python
import functools

import jax
import jax.numpy as jnp
from jax import lax
from jax.experimental import pallas as pl
from jax.experimental.pallas import tpu as pltpu
from jax.sharding import PartitionSpec as P

G = 32
NR, NC = 16, 8
N = NR * NC
HT, WT, C = 16, 128, 256
POS = HT * WT
CAP = 32
epsilon = 1e-06
commit_beta = 0.25
f32, bf16, i32 = jnp.float32, jnp.bfloat16, jnp.int32
MESH = pl.DeviceIdType.MESH
VM = pl.BlockSpec(memory_space=pltpu.VMEM)
SM = pl.BlockSpec(memory_space=pltpu.SMEM)
ANY = pl.BlockSpec(memory_space=pl.ANY)
NT = (((1,), (1,)), ((), ()))


def iota(shape, dim):
    return lax.broadcasted_iota(i32, shape, dim)


COT, QNT, SMO, BCK = 0, 1, 2, 3


def main_kernel(
    lat, ids_s, ids_v, gain, bias, w_enc_hbm, w_dec_hbm, cot_hbm, cb,
    dec_hbm, lg_hbm, gsum_out, wg_out, cg_out,
    dec_out, lg_out,
    S_a, S_q, S_s, hr, hc, hs, colf, cf,
    cbf, qf, slots, idrow, qt, w_enc, w_dec, pull, st,
    msg, stat, sb, rb, idr, dkey, skey,
    grad, p0r, rss, rsr, tb, tr, zr, ag,
    l_sems, h_send, h_recv, s_send, s_recv, i_send, i_recv, c_send, c_recv, p_send, p_recv, g_send, g_recv,
):
    row, col = lax.axis_index("row"), lax.axis_index("col")
    me = row * NC + col
    core = lax.rem(row, 2)
    zed = lax.rem(row // 2, 4)
    ylo = row // 8
    up, dn = lax.rem(row + NR - 1, NR), lax.rem(row + 1, NR)
    lf, rt = lax.rem(col + NC - 1, NC), lax.rem(col + 1, NC)
    count = float(HT * WT * N * (C // G))

    barrier = pltpu.get_barrier_semaphore()

    cols = [col] + [lax.rem(col + c, NC) for c in range(1, NC)]

    def each_peer(act):
        for c in range(1, NC):
            act(row, cols[c])

        def go(r, carry):
            other = lax.rem(row + r, NR)
            for c in range(NC):
                act(other, cols[c])
            return carry

        lax.fori_loop(1, NR, go, 0)

    each_peer(
        lambda r, c: pl.semaphore_signal(barrier, inc=1, device_id={"row": r, "col": c}, device_id_type=MESH)
    )

    def remote(src, dst, ss, rs, dev):
        return pltpu.make_async_remote_copy(
            src_ref=src, dst_ref=dst, send_sem=ss, recv_sem=rs, device_id=dev, device_id_type=MESH
        )

    def drain(ref, sem):
        pltpu.make_async_copy(ref, ref, sem).wait()

    def halo_copies(f, S):
        here = {
            0: (S.at[1, HT], hr.at[f, 0], dn, col),
            1: (S.at[1, 1], hr.at[f, 1], up, col),
            2: (hs.at[f, 1], hc.at[f, 1], row, rt),
            3: (hs.at[f, 1], hc.at[f, 0], dn, rt),
            4: (hs.at[f, 1], hc.at[f, 2], up, rt),
            5: (hs.at[f, 0], hc.at[f, 4], row, lf),
            6: (hs.at[f, 0], hc.at[f, 3], dn, lf),
            7: (hs.at[f, 0], hc.at[f, 5], up, lf),
        }
        return [
            remote(s, d, h_send.at[f, k], h_recv.at[f, k], {"row": r, "col": c})
            for k, (s, d, r, c) in here.items()
        ]

    def halo_send(f, S):
        hs[f] = colf[...].astype(bf16)
        for copy in halo_copies(f, S):
            copy.start()

    ok_u = jnp.where(row > 0, 1.0, 0.0).astype(f32)
    ok_d = jnp.where(row < NR - 1, 1.0, 0.0).astype(f32)
    ok_l = jnp.where(col > 0, 1.0, 0.0).astype(f32)
    ok_r = jnp.where(col < NC - 1, 1.0, 0.0).astype(f32)

    def halo_finish(f, S):
        for copy in halo_copies(f, S):
            copy.wait()
        S[1, 0] = (hr[f, 0].astype(f32) * ok_u).astype(bf16)
        S[1, HT + 1] = (hr[f, 1].astype(f32) * ok_d).astype(bf16)
        for side, ok in ((0, ok_l), (1, ok_r)):
            above = hc[f, 3 * side].astype(f32) * (ok * ok_u)
            below = hc[f, 3 * side + 2].astype(f32) * (ok * ok_d)
            cf[side, 8:24] = hc[f, 3 * side + 1].astype(f32) * ok
            cf[side, 7:8] = above[15:16]
            cf[side, 24:25] = below[0:1]

        def shift(hh, carry):
            v = S[1, hh].astype(f32)
            place = iota((WT, C), 0)
            S[0, hh] = jnp.where(place == 0, cf[0, pl.ds(hh + 7, 1)], pltpu.roll(v, 1, 0)).astype(bf16)
            S[2, hh] = jnp.where(
                place == WT - 1, cf[1, pl.ds(hh + 7, 1)], pltpu.roll(v, WT - 1, 0)
            ).astype(bf16)
            return carry

        lax.fori_loop(0, HT + 2, shift, 0)

    def take_cols(h, v):
        colf[0, pl.ds(h, 1)] = v[0:1]
        colf[1, pl.ds(h, 1)] = v[WT - 1 : WT]

    def field_cols(S):
        def body(h, carry):
            take_cols(h, S[1, h + 1].astype(f32))
            return carry

        lax.fori_loop(0, HT, body, 0)

    BQ, ENC, EB, BA = 0, POS, 2 * POS, 3 * POS

    def put(plane, r0, v):
        cbf[pl.ds(pl.multiple_of(plane + r0 * WT, WT), v.shape[0]), :] = v

    def row_of(plane, h):
        return cbf[pl.ds(pl.multiple_of(plane + h * WT, WT), WT), :]

    RB = 4

    def windows(S, r0, flip):
        parts = []
        for dy in range(3):
            for dx in range(3):
                a, b = (2 - dx, 2 - dy) if flip else (dx, dy)
                parts.append(S[a, pl.ds(r0 + b, RB)].reshape(RB * WT, C))
        return jnp.concatenate(parts, axis=1)

    def conv(S, w, use):
        def body(i, carry):
            r0 = i * RB
            use(r0, jnp.dot(windows(S, r0, False), w[...].reshape(9 * C, C), preferred_element_type=f32))
            return carry

        lax.fori_loop(0, HT // RB, body, 0)

    def convt(S, w, use):
        def body(i, carry):
            r0 = i * RB
            wide = jnp.concatenate([w[k] for k in range(9)], axis=1)
            use(r0, lax.dot_general(windows(S, r0, True), wide, NT, preferred_element_type=f32))
            return carry

        lax.fori_loop(0, HT // RB, body, 0)

    partner = {"row": row + 1 - 2 * core, "col": col}

    here = (lax.rem(col, 4), (col // 4) * 2 + ylo, zed)

    def along(axis, v):
        if axis == 0:
            return {"row": row, "col": (col // 4) * 4 + v}
        if axis == 1:
            return {"row": lax.rem(v, 2) * 8 + lax.rem(row, 8), "col": (v // 2) * 4 + lax.rem(col, 4)}
        return {"row": ylo * 8 + v * 2 + core, "col": col}

    def others(axis, send):
        def go(j, carry):
            t = lax.rem(here[axis] + j, 4)
            send(t, along(axis, t))
            return carry

        lax.fori_loop(1, 4, go, 0)

    def pair0(g, t):
        at = pl.ds(t * 768, 768)
        return remote(grad.at[g, 1 - core, at], p0r.at[g, at], p_send.at[g, t], p_recv.at[g, t], partner)

    def wgrad(g, ut, S):
        for dy in range(3):

            def body(dx, carry, dy=dy):
                win = S[2 - dx, 2 - dy : 2 - dy + HT].reshape(POS, C)
                res = jnp.dot(ut[...], win, preferred_element_type=f32)
                at = pl.ds(pl.multiple_of((dy * 3 + dx) * C, C), C)
                grad[g, 0, at, :] = res[:, :128]
                grad[g, 1, at, :] = res[:, 128:]
                return carry

            lax.fori_loop(0, 3, body, 0)
            pair0(g, dy).start()

    def ar1(g):
        for t in range(3):
            pair0(g, t).wait()

            def add(j, carry, t=t):
                at = pl.ds(pl.multiple_of((t * 4 + j) * 192, 64), 192)
                rss[g, t * 4 + j] = grad[g, core, at, :] + p0r[g, at, :]
                return carry

            lax.fori_loop(0, 4, add, 0)
            mine = t * 4 + here[t]
            rsr[g, mine] = rss[g, mine]
            others(
                t,
                lambda v, dev, t=t, mine=mine: remote(
                    rss.at[g, t * 4 + v], rsr.at[g, mine], g_send.at[g, 1], g_recv.at[g, 1], dev
                ).start(),
            )

    def ar2(g):
        drain(rss.at[g, pl.ds(0, 9)], g_send.at[g, 1])
        drain(rsr.at[g, pl.ds(0, 9)], g_recv.at[g, 1])
        for t in range(3):
            for c in range(4):
                at = slice(c * 48, (c + 1) * 48)
                tb[g, t * 4 + c] = (rsr[g, t * 4, at] + rsr[g, t * 4 + 1, at]) + (
                    rsr[g, t * 4 + 2, at] + rsr[g, t * 4 + 3, at]
                )
        for t in range(3):
            a = (t + 1) % 3
            mine = t * 4 + here[a]
            tr[g, mine] = tb[g, mine]
            others(
                a,
                lambda v, dev, t=t, mine=mine: remote(
                    tb.at[g, t * 4 + v], tr.at[g, mine], g_send.at[g, 2], g_recv.at[g, 2], dev
                ).start(),
            )

    def ar3(g):
        drain(tb.at[g, pl.ds(0, 9)], g_send.at[g, 2])
        drain(tr.at[g, pl.ds(0, 9)], g_recv.at[g, 2])
        for t in range(3):
            a = (t + 2) % 3
            mine = zr.at[g, t * 4 + here[a]]
            zr[g, t * 4 + here[a]] = (tr[g, t * 4] + tr[g, t * 4 + 1]) + (tr[g, t * 4 + 2] + tr[g, t * 4 + 3])
            others(
                a,
                lambda v, dev, mine=mine: remote(mine, mine, g_send.at[g, 3], g_recv.at[g, 3], dev).start(),
            )

    def ar4(g):
        drain(zr.at[g, pl.ds(0, 9)], g_send.at[g, 3])
        drain(zr.at[g, pl.ds(0, 9)], g_recv.at[g, 3])
        for t in range(3):
            a = (t + 1) % 3
            at = t * 16 + here[t] * 4 + here[a]
            ag[g, core, at] = ((zr[g, t * 4] + zr[g, t * 4 + 1]) + (zr[g, t * 4 + 2] + zr[g, t * 4 + 3])).astype(bf16)
            mine = ag.at[g, core, at]
            others(
                a,
                lambda v, dev, mine=mine: remote(mine, mine, g_send.at[g, 4], g_recv.at[g, 4], dev).start(),
            )

    def ar5(g):
        drain(ag.at[g, 0, pl.ds(0, 9)], g_send.at[g, 4])
        drain(ag.at[g, 0, pl.ds(0, 9)], g_recv.at[g, 4])
        for t in range(3):
            mine = ag.at[g, core, pl.ds(t * 16 + here[t] * 4, 4)]
            others(
                t,
                lambda v, dev, mine=mine: remote(mine, mine, g_send.at[g, 5], g_recv.at[g, 5], dev).start(),
            )

    def pair6(g):
        mine = ag.at[g, core]
        return remote(mine, mine, g_send.at[g, 6], g_recv.at[g, 6], partner)

    def ar6(g):
        drain(ag.at[g, 0, pl.ds(0, 36)], g_send.at[g, 5])
        drain(ag.at[g, 0, pl.ds(0, 36)], g_recv.at[g, 5])
        pair6(g).start()

    def ar7(g):
        pair6(g).wait()
        for half in range(2):
            wg_out[g, :, half * 128 : (half + 1) * 128] = ag[g, half].reshape(9 * C, 128)

    def sum_send(a):
        stat[a, me] = msg[a]

        each_peer(
            lambda r, c: remote(
                msg.at[a], stat.at[a, me], s_send.at[a], s_recv.at[a], {"row": r, "col": c}
            ).start()
        )

    def sum_finish(a):
        drain(stat.at[a, pl.ds(0, N - 1)], s_send.at[a])
        drain(stat.at[a, pl.ds(0, N - 1)], s_recv.at[a])
        return jnp.sum(stat[a], axis=0)

    same = (iota((C, C), 0) // (C // G) == iota((C, C), 1) // (C // G)).astype(f32)

    def per_group(v):
        wide = jnp.concatenate([v, jnp.zeros((6, C), f32)], axis=0)
        return jnp.dot(wide, same, precision=lax.Precision.HIGHEST, preferred_element_type=f32)

    parts = cb.shape[0] // HT
    slots_of = [(S_s, 0), (S_s, 1), (S_s, 2), (S_q, 0), (S_q, 1), (S_q, 2)]

    def slot_of(c):
        S, k = slots_of[c % 6]
        return S.at[k, pl.ds(0, HT)]

    def fetch(c):
        return pltpu.make_async_copy(cb.at[pl.ds(c * HT, HT)], slot_of(c), l_sems.at[c % 6])

    cot_copy = pltpu.make_async_copy(cot_hbm, S_a.at[1, pl.ds(1, HT)], l_sems.at[6])
    dec_copy = pltpu.make_async_copy(w_dec_hbm, w_dec, l_sems.at[7])
    enc_copy = pltpu.make_async_copy(w_enc_hbm, w_enc, l_sems.at[8])
    cot_copy.start()
    for c in range(6):
        fetch(c).start()
    dec_copy.start()
    enc_copy.start()

    def first(h, carry):
        v = lat[h].astype(f32)
        return carry[0] + jnp.sum(v, 0, keepdims=True), carry[1] + jnp.sum(v * v, 0, keepdims=True)

    zero = jnp.zeros((1, C), f32)
    s1, s2 = lax.fori_loop(0, HT, first, (zero, zero))
    msg[0, 0:1] = s1
    msg[0, 1:2] = s2
    cot_copy.wait()
    field_cols(S_a)

    upper = (iota((WT, WT), 0) < iota((WT, WT), 1)).astype(f32).astype(bf16)
    base = jnp.zeros((N, 1), f32)
    named = jnp.zeros((N, WT), f32)
    for h in range(HT):
        codes = ids_v[h : h + 1, :]
        member = (iota((N, WT), 0) == (codes >> 7)).astype(f32)
        member_b = member.astype(bf16)
        ahead = jnp.dot(member_b, upper, preferred_element_type=f32)
        slot = jnp.sum(member * (ahead + base), axis=0, keepdims=True)
        base = base + jnp.sum(member, axis=1, keepdims=True)
        slots[h : h + 1, :] = slot
        local = ((codes & 127) + 1).astype(f32)
        lanes = (iota((WT, WT), 0) & (CAP - 1)).astype(f32)
        spread = jnp.where(lanes == slot, local, 0.0).astype(bf16)
        named = named + lax.dot_general(member_b, spread, NT, preferred_element_type=f32)
    idrow[:, 0, :] = named - 1.0

    for c in range(parts):
        fetch(c).wait()
        S, k = slots_of[c % 6]

        def convert(h, carry, c=c, S=S, k=k):
            cbf[pl.ds(pl.multiple_of((c * HT + h) * WT, WT), WT), :] = S[k, h].astype(f32)
            return carry

        lax.fori_loop(0, HT, convert, 0)
        if c + 6 < parts:
            fetch(c + 6).start()

    pl.semaphore_wait(barrier, N - 1)
    sum_send(0)
    halo_send(COT, S_a)
    each_peer(
        lambda r, c: remote(
            idrow.at[r * NC + c], idr.at[me], i_send.at[0], i_recv.at[0], {"row": r, "col": c}
        ).start()
    )
    idr[me] = idrow[me]

    def pick(h, carry):
        def some(t, inner):
            start = h * WT + t * 16
            for j in range(16):
                qf[t, j : j + 1, :] = cbf[pl.ds(ids_s[start + j], 1), :]
            return inner

        lax.fori_loop(0, WT // 16, some, 0)
        v = qf[...].reshape(WT, C)
        S_q[1, h + 1] = v.astype(bf16)
        qt[:, pl.ds(pl.multiple_of(h * WT, WT), WT)] = v.T.astype(bf16)
        take_cols(h, v)
        return carry

    lax.fori_loop(0, HT, pick, 0)
    halo_send(QNT, S_q)

    tot = sum_finish(0)
    grp = per_group(tot)
    mean = grp[0:1] / count
    var = grp[1:2] / count - mean * mean
    inv = lax.rsqrt(var + epsilon)
    gain_v, bias_v = gain[...], bias[...]

    def smoothing(h, carry):
        act = (lat[h].astype(f32) - mean) * inv * gain_v + bias_v
        v = act * jax.nn.sigmoid(act)
        S_s[1, h + 1] = v.astype(bf16)
        st[:, pl.ds(pl.multiple_of(h * WT, WT), WT)] = v.T.astype(bf16)
        take_cols(h, v)
        return carry

    lax.fori_loop(0, HT, smoothing, 0)
    halo_send(SMO, S_s)

    halo_finish(COT, S_a)
    dec_copy.wait()
    enc_copy.wait()
    wgrad(0, qt, S_a)
    convt(S_a, w_dec, lambda r0, v: put(BQ, r0, v))
    halo_finish(SMO, S_s)

    def keep_enc(r0, v):
        put(ENC, r0, v + lat[pl.ds(r0, RB)].reshape(RB * WT, C).astype(f32))

    conv(S_s, w_enc, keep_enc)
    ar1(0)

    def keep_dec(r0, v):
        dec_out[pl.ds(r0, RB)] = v.reshape(RB, WT, C).astype(bf16)

    code_scale = float(16384) / (HT * WT * N)

    def rotate(h, carry):
        for k in range(4):
            at = slice(k * 32, (k + 1) * 32)
            there = pl.ds(pl.multiple_of(h * WT + k * 32, 32), 32)
            z, b = cbf[pl.ds(pl.multiple_of(ENC + h * WT + k * 32, 32), 32), :], cbf[there, :]
            e = S_q[1, h + 1, at].astype(f32)
            z_square = jnp.sum(z * z, -1, keepdims=True) + epsilon
            e_square = jnp.sum(e * e, -1, keepdims=True) + epsilon
            z_over, e_over = lax.rsqrt(z_square), lax.rsqrt(e_square)
            z_unit = z * z_over
            e_unit = e * e_over
            mirror = z_unit + e_unit
            mirror = mirror * lax.rsqrt(jnp.sum(mirror * mirror, -1, keepdims=True) + epsilon)
            along_mirror = jnp.sum(mirror * b, -1, keepdims=True)
            along_code = jnp.sum(e_unit * b, -1, keepdims=True)
            turned = b - (2.0 * along_mirror) * mirror + (2.0 * along_code) * z_unit
            back = (e_square * e_over * z_over) * turned + commit_beta * (z - e)
            cbf[pl.ds(pl.multiple_of(EB + h * WT + k * 32, 32), 32), :] = back
            S_a[1, h + 1, at] = back.astype(bf16)
            pull[there, :] = (code_scale * (e - z)).astype(bf16)
            if k == 0:
                colf[0, pl.ds(h, 1)] = back[0:1]
            if k == 3:
                colf[1, pl.ds(h, 1)] = back[31:32]
        return carry

    lax.fori_loop(0, HT, rotate, 0)
    halo_send(BCK, S_a)
    ar2(0)

    for h in range(HT):
        at = slice(h * WT, (h + 1) * WT)
        dkey[:, at] = jnp.broadcast_to((ids_v[h : h + 1, :] >> 7).astype(f32), (16, WT)).astype(bf16)
        skey[:, at] = jnp.broadcast_to(slots[h : h + 1, :], (16, WT)).astype(bf16)
    low = iota((16, POS), 0).astype(f32).astype(bf16)
    one, nil, gone = jnp.ones((16, POS), bf16), jnp.zeros((16, POS), bf16), jnp.full((16, POS), -1.0, bf16)

    def pack(i, carry):
        first_owner = lax.rem(row + i, NR) * NC
        parts = []
        for j in range(8):
            owner = jnp.full((16, POS), (first_owner + j).astype(f32), f32).astype(bf16)
            key = jnp.where(dkey[...] == owner, skey[...], gone)
            parts.append(jnp.where(key == low, one, nil))
            parts.append(jnp.where(key == low + 16.0, one, nil))
        select = jnp.concatenate(parts, axis=0)
        rows = jnp.dot(select, pull[...], preferred_element_type=f32)
        sb[pl.ds(first_owner, 8)] = rows.reshape(8, CAP, C).astype(bf16)
        return carry

    def send_block(i):
        other = lax.rem(row + i, NR)

        def one_row(c):
            remote(
                sb.at[other * NC + cols[c]], rb.at[me], c_send.at[0], c_recv.at[0], {"row": other, "col": cols[c]}
            ).start()

        @pl.when(i > 0)
        def _():
            one_row(0)

        for c in range(1, NC):
            one_row(c)

    def send_blocks(a, b):
        def go(i, carry):
            send_block(i)
            return carry

        lax.fori_loop(a, b, go, 0)

    def pack_send(i, carry):
        pack(i, carry)
        send_block(i)
        return carry

    lax.fori_loop(0, N // 8, pack_send, 0)

    ar3(0)

    halo_finish(BCK, S_a)
    wgrad(1, st, S_a)
    ar1(1)
    rb[me] = sb[me]
    ar4(0)
    ar2(1)

    def backward(r0, v):
        bs = v.reshape(RB, WT, C)
        s_b, s_g = zero, zero
        for k in range(RB):
            normed = (lat[r0 + k].astype(f32) - mean) * inv
            act = normed * gain_v + bias_v
            s = jax.nn.sigmoid(act)
            t = bs[k] * s * (1.0 + act * (1.0 - s))
            put(BA, r0 + k, t)
            s_b = s_b + jnp.sum(t, 0, keepdims=True)
            s_g = s_g + jnp.sum(t * normed, 0, keepdims=True)
        msg[1, 0:1] += s_b
        msg[1, 1:2] += s_g

    msg[1] = jnp.zeros((2, C), f32)
    convt(S_a, w_enc, backward)
    sum_send(1)
    ar3(1)
    ar5(0)
    halo_finish(QNT, S_q)
    conv(S_q, w_dec, keep_dec)
    dec_back = pltpu.make_async_copy(dec_out, dec_hbm, l_sems.at[9])
    dec_back.start()
    ar4(1)

    tot2 = sum_finish(1)
    gsum_out[...] = tot2
    means = per_group(tot2 * gain_v) * (1.0 / count)
    mean1, mean2 = means[0:1], means[1:2]

    def last(h, carry):
        normed = (lat[h].astype(f32) - mean) * inv
        lg_out[h] = (inv * (row_of(BA, h) * gain_v - mean1 - normed * mean2) + row_of(EB, h)).astype(bf16)
        return carry

    lax.fori_loop(0, HT, last, 0)
    lg_back = pltpu.make_async_copy(lg_out, lg_hbm, l_sems.at[10])
    lg_back.start()
    ar5(1)
    ar6(0)
    drain(idr.at[pl.ds(0, N - 1)], i_send.at[0])
    drain(idr.at[pl.ds(0, N - 1)], i_recv.at[0])
    drain(sb.at[pl.ds(0, N - 1)], c_send.at[0])
    drain(rb.at[pl.ds(0, N - 1)], c_recv.at[0])
    quarter = iota((1, WT), 1) // CAP

    def collect(g, acc):
        hot = []
        for half in range(2):
            names = idr[g * 8 + half * 4]
            for j in range(1, 4):
                names = jnp.where(quarter == j, idr[g * 8 + half * 4 + j], names)
            hot.append((iota((N, WT), 0).astype(f32) == names).astype(f32).astype(bf16))
        rows = rb[pl.ds(g * 8, 8)].reshape(8 * CAP, C)
        return acc + jnp.dot(jnp.concatenate(hot, axis=1), rows, preferred_element_type=f32)

    cg_out[...] = lax.fori_loop(0, N // 8, collect, jnp.zeros((N, C), f32))
    ar6(1)
    ar7(0)

    ar7(1)
    dec_back.wait()
    lg_back.wait()


def main(lat, code_ids, gain, bias, w_enc, w_dec, cot, codebook):
    dma = pltpu.SemaphoreType.DMA
    V = pltpu.VMEM
    field = V((3, HT + 2, WT, C), bf16)
    return pl.pallas_call(
        main_kernel,
        out_shape=(
            jax.ShapeDtypeStruct((HT, WT, C), bf16),
            jax.ShapeDtypeStruct((HT, WT, C), bf16),
            jax.ShapeDtypeStruct((2, C), f32),
            jax.ShapeDtypeStruct((2, 9 * C, C), bf16),
            jax.ShapeDtypeStruct((N, C), f32),
        ),
        in_specs=[VM, SM, VM, VM, VM, ANY, ANY, ANY, ANY],
        out_specs=(ANY, ANY, VM, VM, VM),
        scratch_shapes=[
            V((HT, WT, C), bf16), V((HT, WT, C), bf16),
            field, field, field,
            V((4, 2, WT, C), bf16), V((4, 6, HT, C), bf16), V((4, 2, HT, C), bf16),
            V((2, HT, C), f32), V((2, 32, C), f32),
            V((codebook.shape[0] * WT, C), f32), V((WT // 16, 16, C), f32), V((HT, WT), f32),
            V((N, 1, WT), f32), V((C, POS), bf16), V((9, C, C), bf16), V((9, C, C), bf16),
            V((POS, C), bf16), V((C, POS), bf16),
            V((2, 2, C), f32), V((2, N, 2, C), f32),
            V((N, CAP, C), bf16), V((N, CAP, C), bf16), V((N, 1, WT), f32),
            V((16, POS), bf16), V((16, POS), bf16),
            V((2, 2, 9 * C, 128), f32), V((2, 9 * C, 128), f32),
            V((2, 12, 192, 128), f32), V((2, 12, 192, 128), f32), V((2, 12, 48, 128), f32), V((2, 12, 48, 128), f32),
            V((2, 12, 48, 128), f32), V((2, 2, 48, 48, 128), bf16),
            dma((11,)), dma((4, 8)), dma((4, 8)), dma((2,)), dma((2,)), dma((1,)), dma((1,)), dma((1,)), dma((1,)),
            dma((2, 3)), dma((2, 3)), dma((2, 7)), dma((2, 7)),
        ],
        compiler_params=pltpu.CompilerParams(
            collective_id=0, has_side_effects=True, vmem_limit_bytes=67_000_000
        ),
        name="main",
    )(lat, code_ids.reshape(POS), code_ids, gain, bias, w_enc, w_dec, cot, codebook)


def body(latents, code_ids, norm_gain, norm_bias, encoder_weight, codebook, decoder_weight, cotangent):
    decoded, latents_grad, gsum, wg, cg = main(
        latents, code_ids, norm_gain.reshape(1, C), norm_bias.reshape(1, C),
        encoder_weight.reshape(9, C, C), decoder_weight.reshape(9, C, C), cotangent, codebook.reshape(-1, WT, C),
    )
    wg = wg.reshape(2, 3, 3, C, C).astype(f32)
    return decoded, latents_grad, gsum[1], gsum[0], wg[1], wg[0], cg


def solution(mesh):
    tiled = P("row", "col", None)
    in_specs = (tiled, P("row", "col"), P(), P(), P(), P(), P(), tiled)
    out_specs = (tiled, tiled, P(), P(), P(), P(), P(("row", "col"), None))
    return jax.shard_map(body, mesh=mesh, in_specs=in_specs, out_specs=out_specs, check_vma=False)
```
